256 devices in a mesh: fsdp: 16 (over y, x), ctx: 16 (over z, core).
Axes of the slice: x: 4, y: 4, z: 8, core: 2. Of those that a mesh axis runs over, the one named last changes fastest.
Arguments:
- queries: bfloat16 [32768, 2048], P(('fsdp', 'ctx')), may hold values from -80 to 80
- keys: bfloat16 [32768, 2048], P(('fsdp', 'ctx')), may hold values from -4 to 4
- values: bfloat16 [32768, 2048], P(('fsdp', 'ctx')), may hold values from -6 to 6
- out_weight: bfloat16 [2048, 4096], P('fsdp'), may hold values from -0.125 to 0.125
- sessions: int32 [16, 2048], P('fsdp'), may hold values from 0 to 2, never falling along the last dimension, each value on 1 to 1536 neighbouring positions
Outputs:
- output: bfloat16 [32768, 4096], P(('fsdp', 'ctx'))
The draws below stay inside these ranges and needn't reach their ends.
Inputs may be any that keep to these rules, and one draw needn't show every extreme that they name: Along each slab the session number never falls; each of the 3 sessions holds 1 to 1536 tokens and one holds exactly 1536.
All inputs are finite; a program needn't handle non-finite values.
Results may differ from the reference program's by a relative error of at most 0.007.
Values may be sent and summed in bfloat16 or wider, within the bound.
No kernel may reach another device: no remote copies, remote signals or barrier semaphores. Data moves between devices by JAX's collectives and lax.ppermute only.
A program may use at most 128 MiB of HBM per device.

```python
import math
import jax
import jax.numpy as jnp
import numpy as np
from jax import lax

D = 4096
HEADS = 16
HDIM = 128
SESS = 3
SLAB = 2048
MOST = 1536
TOKENS = 32768
N_FSDP = 16


def query_key_pair(key):
    folded = jax.random.fold_in(key, 7)
    key_one, key_two = jax.random.split(folded, 2)
    width = HEADS * HDIM
    key_rows = jnp.clip(jax.random.normal(key_one, (TOKENS, width), jnp.float32), -4.0, 4.0)
    query_rows = jnp.clip(jax.random.normal(key_two, (TOKENS, width), jnp.float32), -4.0, 4.0)
    return (query_rows, key_rows)


def draw_queries(key, part):
    return query_key_pair(key)[0].astype(jnp.bfloat16)


def draw_keys(key, part):
    return query_key_pair(key)[1].astype(jnp.bfloat16)


def steps_of(own_key, shape, pieces, smallest, top_value):
    loudness, own = 1.0, jax.random.fold_in(own_key, 6)
    for dim, parts in pieces:
        draws = jnp.exp(jax.random.uniform(jax.random.fold_in(own, dim), (parts,), jnp.float32, smallest / len(pieces), top_value / len(pieces)))
        loudness = loudness * jnp.repeat(draws, shape[dim] // parts).reshape([-1 if axis == dim else 1 for axis in range(len(shape))])
    return loudness


def length_profile(number_of, total, limit, lean):
    weights = [(1 << 20) // math.isqrt(rank ** lean) + 1 for rank in range(2, number_of + 1)]
    rest, given = total - limit - (number_of - 1), [1] * (number_of - 1)
    while rest > 0:
        movable = [i for i in range(number_of - 1) if given[i] < limit]
        mass, left = sum([weights[i] for i in movable]), rest
        for i in movable:
            extra = min(limit - given[i], max(1, left * weights[i] // mass), rest)
            given[i] = given[i] + extra
            rest = rest - extra
    return np.array([limit] + given)


def ragged(key, number_of, total, reach, skew):
    if number_of == 2:
        one = jax.random.randint(key, (), max(1, total - reach), min(reach, total - 1) + 1)
        return jnp.stack([one, total - one])
    tallies = jnp.asarray(length_profile(number_of, total, reach, skew), jnp.int32)
    pairs = (number_of - 1) // 2
    donor, sink = tallies[1:1 + 2 * pairs:2], tallies[2:2 + 2 * pairs:2]
    slack = jnp.minimum(donor - 1, reach - sink)
    moved = jax.random.randint(jax.random.fold_in(key, 1), (pairs,), 0, 1 << 20) % (slack + 1)
    tallies = tallies.at[1:1 + 2 * pairs:2].set(donor - moved).at[2:2 + 2 * pairs:2].set(sink + moved)
    return tallies[jax.random.permutation(jax.random.fold_in(key, 2), number_of)]


def bell_draw(rng, extent, spread, most, shards=(), held_as=jnp.bfloat16):
    result = spread * jax.random.normal(rng, extent, jnp.float32)
    if shards:
        result = result * steps_of(rng, extent, shards, -0.22, 0.18)
    return jnp.clip(result, -most, most).astype(held_as)


def setup_inputs(seed: int = 0) -> dict:
    key_of = jax.random.split(jax.random.key(seed), 6)
    queries = draw_queries(jax.random.fold_in(key_of[5], 71), 0)
    keys = draw_keys(jax.random.fold_in(key_of[5], 71), 0)
    values = bell_draw(key_of[2], (TOKENS, HEADS * HDIM), 1.0, 6.0, ((0, 256),))
    out_weight = bell_draw(key_of[3], (HEADS * HDIM, D), (HEADS * HDIM) ** -0.5, 0.125, ((0, 16),))
    sessions = jax.vmap(lambda own: jnp.searchsorted(jnp.cumsum(ragged(own, SESS, SLAB, MOST, 1)), jnp.arange(SLAB), side="right"))(jax.random.split(key_of[4], N_FSDP)).reshape((N_FSDP, SLAB)).astype(jnp.int32)
    return dict(queries=queries, keys=keys, values=values, out_weight=out_weight, sessions=sessions)


def head_attention(operands):
    query_head, key_head, value_head, allowed = operands
    scale = 1.0 / math.sqrt(HDIM)
    scores = jnp.dot(query_head, key_head.T, preferred_element_type=jnp.float32) * scale
    scores = jnp.where(allowed, scores, jnp.float32(-1e+30))
    row_max = lax.optimization_barrier(jnp.max(scores, axis=1, keepdims=True))
    weights = jnp.where(allowed, jnp.exp(scores - row_max), jnp.float32(0.0))
    total = lax.optimization_barrier(jnp.sum(weights, axis=1, keepdims=True))
    summed = jnp.dot(weights.astype(jnp.bfloat16), value_head, preferred_element_type=jnp.float32)
    return summed / total

def one_slab(operands):
    query_slab, key_slab, value_slab, slab_ids = operands
    positions = jnp.arange(SLAB, dtype=jnp.int32)
    allowed = (slab_ids[:, None] == slab_ids[None, :]) & (positions[None, :] <= positions[:, None])
    query_heads = jnp.transpose(query_slab.reshape(SLAB, HEADS, HDIM), (1, 0, 2))
    key_heads = jnp.transpose(key_slab.reshape(SLAB, HEADS, HDIM), (1, 0, 2))
    value_heads = jnp.transpose(value_slab.reshape(SLAB, HEADS, HDIM), (1, 0, 2))
    results = lax.map(lambda triple: head_attention((triple[0], triple[1], triple[2], allowed)), (query_heads, key_heads, value_heads))
    return jnp.transpose(results, (1, 0, 2)).reshape(SLAB, HEADS * HDIM).astype(jnp.bfloat16)

def reference(queries, keys, values, out_weight, sessions):
    width = HEADS * HDIM
    attended = lax.map(one_slab, (queries.reshape(N_FSDP, SLAB, width), keys.reshape(N_FSDP, SLAB, width), values.reshape(N_FSDP, SLAB, width), sessions))
    attended = attended.reshape(TOKENS, width)
    return jnp.dot(attended, out_weight, preferred_element_type=jnp.float32).astype(jnp.bfloat16)
```

```python
import math

import jax
import jax.numpy as jnp
from jax import lax
from jax.experimental import pallas as pl
from jax.experimental.pallas import tpu as pltpu
from jax.sharding import PartitionSpec as P

HDIM = 128
Q_TILE = 256
K_TILE = 512
MASKED = -1e30


def attention_kernel(bounds_ref, q_ref, k_ref, v_ref, out_ref):
    blocks, rows, _ = q_ref.shape
    first, second = bounds_ref[0], bounds_ref[1]
    factor = math.log2(math.e) / math.sqrt(HDIM)

    def start_of(position):
        return jnp.where(position >= second, second, jnp.where(position >= first, first, 0))

    for tile in range(blocks * rows // Q_TILE):
        q_blocks = slice(tile * Q_TILE // rows, (tile + 1) * Q_TILE // rows)
        q_tile = q_ref[q_blocks].reshape(Q_TILE, HDIM)
        q_pos = tile * Q_TILE + lax.broadcasted_iota(jnp.int32, (1, Q_TILE), 1)
        q_start = start_of(q_pos)
        low = start_of(jnp.int32(tile * Q_TILE)) // K_TILE
        high = (tile * Q_TILE + Q_TILE - 1) // K_TILE + 1

        def step(j, carry):
            row_max, total, accum = carry
            k_blocks = pl.ds(j * (K_TILE // rows), K_TILE // rows)
            k_tile = k_ref[k_blocks].reshape(K_TILE, HDIM)
            v_tile = v_ref[k_blocks].reshape(K_TILE, HDIM)
            scores = lax.dot_general(
                k_tile, q_tile, (((1,), (1,)), ((), ())), preferred_element_type=jnp.float32
            )
            k_pos = j * K_TILE + lax.broadcasted_iota(jnp.int32, (K_TILE, 1), 0)
            allowed = (k_pos >= q_start) & (k_pos <= q_pos)
            scores = jnp.where(allowed, scores, MASKED)
            new_max = jnp.maximum(row_max, jnp.max(scores, axis=0, keepdims=True))
            weights = jnp.where(allowed, jnp.exp2((scores - new_max) * factor), 0.0)
            rescale = jnp.exp2((row_max - new_max) * factor)
            new_total = total * rescale + jnp.sum(weights, axis=0, keepdims=True)
            added = lax.dot_general(
                v_tile,
                weights.astype(jnp.bfloat16),
                (((0,), (0,)), ((), ())),
                preferred_element_type=jnp.float32,
            )
            return new_max, new_total, accum * rescale + added

        start_state = (
            jnp.full((1, Q_TILE), MASKED, jnp.float32),
            jnp.zeros((1, Q_TILE), jnp.float32),
            jnp.zeros((HDIM, Q_TILE), jnp.float32),
        )
        _, total, accum = lax.fori_loop(low, high, step, start_state)
        finished = jnp.transpose(accum / total).astype(jnp.bfloat16)
        out_ref[q_blocks] = finished.reshape(Q_TILE // rows, rows, HDIM)


def head_attention(bounds, packed):
    blocks, _, rows, _ = packed.shape

    def part(index):
        return pl.BlockSpec((blocks, None, rows, HDIM), lambda i, b: (0, index, 0, 0))

    return pl.pallas_call(
        attention_kernel,
        out_shape=jax.ShapeDtypeStruct((blocks, rows, HDIM), jnp.bfloat16),
        grid_spec=pltpu.PrefetchScalarGridSpec(
            num_scalar_prefetch=1,
            grid=(1,),
            in_specs=[part(0), part(1), part(2)],
            out_specs=pl.BlockSpec((blocks, rows, HDIM), lambda i, b: (0, 0, 0)),
        ),
        compiler_params=pltpu.CompilerParams(vmem_limit_bytes=40 << 20),
        name="head_attention",
    )(bounds, packed, packed, packed)


def per_device(queries, keys, values, out_weight, sessions):
    rows, width = queries.shape
    heads = width // HDIM
    half = out_weight.shape[1] // 2
    core = lax.axis_index("ctx") % 2
    swap = [(i, i ^ 1) for i in range(lax.axis_size("ctx"))]
    my_columns = lax.dynamic_slice_in_dim(out_weight, core * half, half, 1)
    weight = lax.all_gather(my_columns, "fsdp", axis=0, tiled=True)
    bounds = jnp.stack([jnp.sum(sessions[0] < 1), jnp.sum(sessions[0] < 2)]).astype(jnp.int32)

    packed = jnp.concatenate([queries, keys, values], axis=0)
    packed = lax.all_to_all(packed, "ctx", 1, 0, tiled=True)
    attended = head_attention(bounds, packed.reshape(heads, 3, rows, HDIM))
    attended = lax.all_to_all(attended, "ctx", 0, 0, tiled=True)
    mine = jnp.transpose(attended, (1, 0, 2)).reshape(rows, width)
    theirs = lax.ppermute(mine, "ctx", swap)
    projected = jnp.dot(
        jnp.concatenate([mine, theirs], axis=0), weight, preferred_element_type=jnp.float32
    ).astype(jnp.bfloat16)
    kept = projected[:rows]
    got = lax.ppermute(projected[rows:], "ctx", swap)
    left = jnp.where(core == 0, kept, got)
    right = jnp.where(core == 0, got, kept)
    return jnp.concatenate([left, right], axis=1)


def solution(mesh):
    return jax.shard_map(
        per_device,
        mesh=mesh,
        in_specs=(
            P(("fsdp", "ctx"), None),
            P(("fsdp", "ctx"), None),
            P(("fsdp", "ctx"), None),
            P("fsdp", None),
            P("fsdp", None),
        ),
        out_specs=P(("fsdp", "ctx"), None),
        check_vma=False,
    )
```

```python
import functools
import math

import jax
import jax.numpy as jnp
from jax import lax
from jax.experimental import pallas as pl
from jax.experimental.pallas import tpu as pltpu
from jax.sharding import PartitionSpec as P

HDIM = 128
Q_TILE = 256
K_TILE = 512
MASKED = -1e30
SIDE = 4
NEAR = (0, 1, 3, 2)


def attention_kernel(bounds_ref, q_ref, k_ref, v_ref, out_ref):
    blocks, rows, _ = q_ref.shape
    first, second = bounds_ref[0], bounds_ref[1]
    factor = math.log2(math.e) / math.sqrt(HDIM)

    def start_of(position):
        return jnp.where(position >= second, second, jnp.where(position >= first, first, 0))

    for tile in range(blocks * rows // Q_TILE):
        q_blocks = slice(tile * Q_TILE // rows, (tile + 1) * Q_TILE // rows)
        q_tile = q_ref[q_blocks].reshape(Q_TILE, HDIM)
        q_pos = tile * Q_TILE + lax.broadcasted_iota(jnp.int32, (1, Q_TILE), 1)
        q_start = start_of(q_pos)
        low = start_of(jnp.int32(tile * Q_TILE)) // K_TILE
        high = (tile * Q_TILE + Q_TILE - 1) // K_TILE + 1

        def step(j, carry):
            row_max, total, accum = carry
            k_blocks = pl.ds(j * (K_TILE // rows), K_TILE // rows)
            k_tile = k_ref[k_blocks].reshape(K_TILE, HDIM)
            v_tile = v_ref[k_blocks].reshape(K_TILE, HDIM)
            scores = lax.dot_general(
                k_tile, q_tile, (((1,), (1,)), ((), ())), preferred_element_type=jnp.float32
            )
            k_pos = j * K_TILE + lax.broadcasted_iota(jnp.int32, (K_TILE, 1), 0)
            allowed = (k_pos >= q_start) & (k_pos <= q_pos)
            scores = jnp.where(allowed, scores, MASKED)
            new_max = jnp.maximum(row_max, jnp.max(scores, axis=0, keepdims=True))
            weights = jnp.where(allowed, jnp.exp2((scores - new_max) * factor), 0.0)
            rescale = jnp.exp2((row_max - new_max) * factor)
            new_total = total * rescale + jnp.sum(weights, axis=0, keepdims=True)
            added = lax.dot_general(
                v_tile,
                weights.astype(jnp.bfloat16),
                (((0,), (0,)), ((), ())),
                preferred_element_type=jnp.float32,
            )
            return new_max, new_total, accum * rescale + added

        start_state = (
            jnp.full((1, Q_TILE), MASKED, jnp.float32),
            jnp.zeros((1, Q_TILE), jnp.float32),
            jnp.zeros((HDIM, Q_TILE), jnp.float32),
        )
        _, total, accum = lax.fori_loop(low, high, step, start_state)
        finished = jnp.transpose(accum / total).astype(jnp.bfloat16)
        out_ref[q_blocks] = finished.reshape(Q_TILE // rows, rows, HDIM)


def pack_kernel(queries_ref, keys_ref, values_ref, out_ref):
    for index, ref in enumerate((queries_ref, keys_ref, values_ref)):
        for head in range(out_ref.shape[0]):
            out_ref[head, index] = ref[:, head * HDIM:(head + 1) * HDIM]


def pack(queries, keys, values):
    rows, width = queries.shape
    return pl.pallas_call(
        pack_kernel,
        out_shape=jax.ShapeDtypeStruct((width // HDIM, 3, rows, HDIM), queries.dtype),
        name="pack",
    )(queries, keys, values)


def head_attention(bounds, packed):
    blocks, _, rows, _ = packed.shape

    def part(index):
        return pl.BlockSpec((blocks, None, rows, HDIM), lambda i, b: (0, index, 0, 0))

    return pl.pallas_call(
        attention_kernel,
        out_shape=jax.ShapeDtypeStruct((blocks, rows, HDIM), jnp.bfloat16),
        grid_spec=pltpu.PrefetchScalarGridSpec(
            num_scalar_prefetch=1,
            grid=(1,),
            in_specs=[part(0), part(1), part(2)],
            out_specs=pl.BlockSpec((blocks, rows, HDIM), lambda i, b: (0, 0, 0)),
        ),
        compiler_params=pltpu.CompilerParams(vmem_limit_bytes=12 << 20),
        name="head_attention",
    )(bounds, packed, packed, packed)


def projection_kernel(offsets, place_ref, mine_ref, theirs_ref, *rest):
    pieces, (kept_ref, sent_ref, left_ref) = list(rest[:-3]), rest[-3:]
    rows = mine_ref.shape[1]
    columns = pieces[0].shape[2]
    y, x = place_ref[0], place_ref[1]
    for side, lists in enumerate(offsets):
        accum = None
        start = 0
        for places in lists:
            for dy, dx in places:
                head = ((y + dy + SIDE) % SIDE) * SIDE + (x + dx + SIDE) % SIDE
                left_ref[:rows, start:start + HDIM] = mine_ref[head]
                left_ref[rows:, start:start + HDIM] = theirs_ref[head]
                start += HDIM
        start = 0
        for places in lists:
            depth = len(places) * HDIM
            piece = pieces.pop(0)[...].reshape(depth, columns)
            added = jnp.dot(left_ref[:, start:start + depth], piece, preferred_element_type=jnp.float32)
            accum = added if accum is None else accum + added
            start += depth
        result = accum.astype(jnp.bfloat16)
        kept_ref[:, side * columns:(side + 1) * columns] = result[:rows]
        sent_ref[:, side * columns:(side + 1) * columns] = result[rows:]


def project(place, mine, theirs, pieces, offsets):
    heads, rows, _ = mine.shape
    columns = 2 * pieces[0].shape[2]
    vmem = pl.BlockSpec(memory_space=pltpu.VMEM)
    out = jax.ShapeDtypeStruct((rows, columns), jnp.bfloat16)
    return pl.pallas_call(
        functools.partial(projection_kernel, offsets),
        out_shape=(out, out),
        in_specs=[pl.BlockSpec(memory_space=pltpu.SMEM)] + [vmem] * (2 + len(pieces)),
        out_specs=(vmem, vmem),
        scratch_shapes=[pltpu.VMEM((2 * rows, heads * HDIM), jnp.bfloat16)],
        compiler_params=pltpu.CompilerParams(vmem_limit_bytes=10 << 20),
        name="project",
    )(place, mine, theirs, *pieces)


def fetch(piece, dy, dx):
    pairs = [
        (SIDE * ((y + dy + SIDE) % SIDE) + (x + dx) % SIDE, SIDE * y + x)
        for y in range(SIDE)
        for x in range(SIDE)
    ]
    return lax.ppermute(piece, "fsdp", pairs)


def per_device(queries, keys, values, out_weight, sessions):
    core = lax.axis_index("ctx") % 2
    swap = [(i, i ^ 1) for i in range(lax.axis_size("ctx"))]
    bounds = jnp.stack([jnp.sum(sessions[0] < 1), jnp.sum(sessions[0] < 2)]).astype(jnp.int32)
    place = lax.axis_index("fsdp")
    place = jnp.stack([place // SIDE, place % SIDE]).astype(jnp.int32)

    packed = lax.all_to_all(pack(queries, keys, values), "ctx", 0, 0, tiled=True)

    half = out_weight.shape[1] // 2
    first = lax.dynamic_slice_in_dim(out_weight, core * half, half // 2, 1)
    second = lax.dynamic_slice_in_dim(out_weight, core * half + half // 2, half // 2, 1)
    first = jnp.stack([first] + [fetch(first, 0, step) for step in NEAR[1:]])
    second = jnp.stack([second] + [fetch(second, step, 0) for step in NEAR[1:]])
    packed, _, _ = lax.optimization_barrier((packed, first, second))
    beside = [fetch(first, 1, 0), fetch(first, -1, 0), fetch(second, 0, 1), fetch(second, 0, -1)]

    attended = head_attention(bounds, packed)
    attended, *_ = lax.optimization_barrier((attended, *beside))
    far = [
        fetch(beside[0][:2], 1, 0),
        fetch(beside[1][2:], -1, 0),
        fetch(beside[2][:2], 0, 1),
        fetch(beside[3][2:], 0, -1),
    ]
    pieces = [first, beside[0], beside[1], far[0], far[1], second, beside[2], beside[3], far[2], far[3]]
    steps = [(0, NEAR), (1, NEAR), (-1, NEAR), (2, NEAR[:2]), (2, NEAR[2:])]
    offsets = (
        [[(dy, dx) for dx in near] for dy, near in steps],
        [[(dy, dx) for dy in near] for dx, near in steps],
    )

    mine = lax.all_to_all(attended, "ctx", 0, 0, tiled=True)
    theirs = lax.ppermute(mine, "ctx", swap)
    kept, sent = project(place, mine, theirs, pieces, offsets)
    got = lax.ppermute(sent, "ctx", swap)
    left = jnp.where(core == 0, kept, got)
    right = jnp.where(core == 0, got, kept)
    return jnp.concatenate([left, right], axis=1)


def solution(mesh):
    return jax.shard_map(
        per_device,
        mesh=mesh,
        in_specs=(
            P(("fsdp", "ctx"), None),
            P(("fsdp", "ctx"), None),
            P(("fsdp", "ctx"), None),
            P("fsdp", None),
            P("fsdp", None),
        ),
        out_specs=P(("fsdp", "ctx"), None),
        check_vma=False,
    )
```

```python
import functools
import math

import jax
import jax.numpy as jnp
from jax import lax
from jax.experimental import pallas as pl
from jax.experimental.pallas import tpu as pltpu
from jax.sharding import PartitionSpec as P

HDIM = 128
TILE = 512
CHAIN = 256
MASKED = -1e30
SIDE = 4
NEAR = (0, 1, 3, 2)


def attention_kernel(bounds_ref, packed_ref, out_ref, vt_ref):
    blocks, _, rows, _ = packed_ref.shape
    slab = blocks * rows
    first, second = bounds_ref[0], bounds_ref[1]
    factor = math.log2(math.e) / math.sqrt(HDIM)
    chains = TILE // CHAIN

    def start_of(position):
        return jnp.where(position >= second, second, jnp.where(position >= first, first, 0))

    def tokens(index, start, count):
        return packed_ref[pl.ds(start // rows, count // rows), index].reshape(count, HDIM)

    for block in range(blocks):
        vt_ref[block] = jnp.transpose(packed_ref[block, 2])

    def values_t(start, count):
        part = vt_ref[pl.ds(start // rows, count // rows)]
        return jnp.concatenate([part[i] for i in range(count // rows)], axis=1)

    def attend(state, query, keys, v_t, mask):
        scores = lax.dot_general(keys, query, (((1,), (1,)), ((), ())), preferred_element_type=jnp.float32)
        if mask is not None:
            scores = jnp.where(mask, scores, MASKED)
        top = jnp.max(scores, axis=0, keepdims=True)
        if state is not None:
            top = jnp.maximum(state[0], top)
        weights = jnp.exp2((scores - top) * factor)
        total = jnp.sum(weights, axis=0, keepdims=True)
        accum = jnp.dot(v_t, weights.astype(jnp.bfloat16), preferred_element_type=jnp.float32)
        if state is not None:
            rescale = jnp.exp2((state[0] - top) * factor)
            total = total + state[1] * rescale
            accum = accum + state[2] * rescale
        return top, total, accum

    for tile in range(slab // TILE):
        base = tile * TILE
        queries, positions, starts, states = [], [], [], []
        for chain in range(chains):
            at = base + chain * CHAIN
            queries.append(tokens(0, at, CHAIN))
            position = at + lax.broadcasted_iota(jnp.int32, (1, CHAIN), 1)
            starts.append(start_of(position))
            count = (chain + 1) * CHAIN
            key_pos = base + lax.broadcasted_iota(jnp.int32, (count, 1), 0)
            mask = (key_pos <= position) & (key_pos >= starts[-1])
            states.append(attend(None, queries[-1], tokens(1, base, count), values_t(base, count), mask))
        if tile:
            low = start_of(jnp.int32(base)) // TILE
            full = jnp.minimum((start_of(jnp.int32(base + TILE - 1)) + TILE - 1) // TILE, tile)

            def step(masked, j, states):
                start = pl.multiple_of(j * TILE, TILE)
                keys, v_t = tokens(1, start, TILE), values_t(start, TILE)
                out = []
                for chain in range(chains):
                    mask = None
                    if masked:
                        mask = start + lax.broadcasted_iota(jnp.int32, (TILE, 1), 0) >= starts[chain]
                    out.append(attend(states[chain], queries[chain], keys, v_t, mask))
                return tuple(out)

            states = lax.fori_loop(full, tile, lambda j, s: step(False, j, s), tuple(states))
            states = lax.fori_loop(low, full, lambda j, s: step(True, j, s), states)
        for chain in range(chains):
            _, total, accum = states[chain]
            finished = jnp.transpose((accum / total).astype(jnp.bfloat16))
            at = (base + chain * CHAIN) // rows
            out_ref[at:at + CHAIN // rows] = finished.reshape(CHAIN // rows, rows, HDIM)


def pack_kernel(queries_ref, keys_ref, values_ref, out_ref, semaphores):
    copies = []
    for head in range(out_ref.shape[0]):
        for index, ref in enumerate((queries_ref, keys_ref, values_ref)):
            source = ref.at[:, head * HDIM:(head + 1) * HDIM]
            copies.append(
                pltpu.make_async_copy(source, out_ref.at[head, index], semaphores.at[head, index])
            )
    for copy in copies:
        copy.start()
    for copy in copies:
        copy.wait()


def pack(queries, keys, values):
    rows, width = queries.shape
    hbm = pl.BlockSpec(memory_space=pl.ANY)
    return pl.pallas_call(
        pack_kernel,
        out_shape=jax.ShapeDtypeStruct((width // HDIM, 3, rows, HDIM), queries.dtype),
        in_specs=[hbm] * 3,
        out_specs=hbm,
        scratch_shapes=[pltpu.SemaphoreType.DMA((width // HDIM, 3))],
        name="pack",
    )(queries, keys, values)


def head_attention(bounds, packed):
    blocks, _, rows, _ = packed.shape
    vmem = pl.BlockSpec(memory_space=pltpu.VMEM)
    return pl.pallas_call(
        attention_kernel,
        out_shape=jax.ShapeDtypeStruct((blocks, rows, HDIM), jnp.bfloat16),
        in_specs=[pl.BlockSpec(memory_space=pltpu.SMEM), vmem],
        out_specs=vmem,
        scratch_shapes=[pltpu.VMEM((blocks, HDIM, rows), jnp.bfloat16)],
        compiler_params=pltpu.CompilerParams(vmem_limit_bytes=16 << 20),
        name="head_attention",
    )(bounds, packed)


def projection_kernel(offsets, place_ref, mine_ref, theirs_ref, *rest):
    pieces, (out_ref, sent_ref, kept_ref, left_ref, weight_ref, semaphores) = rest[:-6], rest[-6:]
    columns = pieces[0].shape[2]
    rows = mine_ref.shape[1]
    y, x, core = place_ref[0], place_ref[1], place_ref[2]
    copies, kept_copies = [], []
    at = 0
    for index, piece in enumerate(pieces):
        steps = piece.shape[0]
        copies.append(
            pltpu.make_async_copy(piece, weight_ref.at[pl.ds(at, steps)], semaphores.at[index])
        )
        copies[-1].start()
        at += steps
    at = 0
    for side, lists in enumerate(offsets):
        accum = None
        start = 0
        for places in lists:
            for dy, dx in places:
                head = ((y + dy + SIDE) % SIDE) * SIDE + (x + dx + SIDE) % SIDE
                left_ref[:rows, start:start + HDIM] = mine_ref[head]
                left_ref[rows:, start:start + HDIM] = theirs_ref[head]
                start += HDIM
        start = 0
        for places in lists:
            depth = len(places) * HDIM
            copies.pop(0).wait()
            piece = weight_ref[at:at + len(places)].reshape(depth, columns)
            added = jnp.dot(left_ref[:, start:start + depth], piece, preferred_element_type=jnp.float32)
            accum = added if accum is None else accum + added
            start += depth
            at += len(places)
        result = accum.astype(jnp.bfloat16)
        sent_ref[:, side * columns:(side + 1) * columns] = result[rows:]
        kept_ref[side] = result[:rows]
        target = out_ref.at[:, pl.ds(pl.multiple_of((2 * core + side) * columns, columns), columns)]
        kept_copies.append(
            pltpu.make_async_copy(kept_ref.at[side], target, semaphores.at[len(pieces) + side])
        )
        kept_copies[-1].start()
    for copy in kept_copies:
        copy.wait()


def project(place, mine, theirs, pieces, offsets):
    heads, rows, _ = mine.shape
    columns = pieces[0].shape[2]
    vmem = pl.BlockSpec(memory_space=pltpu.VMEM)
    hbm = pl.BlockSpec(memory_space=pltpu.HBM)
    return pl.pallas_call(
        functools.partial(projection_kernel, offsets),
        out_shape=(
            jax.ShapeDtypeStruct((rows, 4 * columns), jnp.bfloat16),
            jax.ShapeDtypeStruct((rows, 2 * columns), jnp.bfloat16),
        ),
        in_specs=[pl.BlockSpec(memory_space=pltpu.SMEM), vmem, vmem]
        + [hbm] * len(pieces),
        out_specs=(hbm, vmem),
        scratch_shapes=[
            pltpu.VMEM((2, rows, columns), jnp.bfloat16),
            pltpu.VMEM((2 * rows, heads * HDIM), jnp.bfloat16),
            pltpu.VMEM((2 * heads, HDIM, columns), jnp.bfloat16),
            pltpu.SemaphoreType.DMA((len(pieces) + 2,)),
        ],
        compiler_params=pltpu.CompilerParams(vmem_limit_bytes=20 << 20),
        name="project",
    )(place, mine, theirs, *[pltpu.with_memory_space_constraint(piece, pltpu.HBM) for piece in pieces])


def join_kernel(place_ref, got_ref, part_ref, out_ref, semaphore):
    half = got_ref.shape[1]
    other = pl.multiple_of((1 - place_ref[2]) * half, half)
    copy = pltpu.make_async_copy(got_ref, out_ref.at[:, pl.ds(other, half)], semaphore)
    copy.start()
    copy.wait()


def join(place, got, part):
    hbm = pl.BlockSpec(memory_space=pltpu.HBM)
    return pl.pallas_call(
        join_kernel,
        out_shape=jax.ShapeDtypeStruct(part.shape, part.dtype),
        in_specs=[pl.BlockSpec(memory_space=pltpu.SMEM), pl.BlockSpec(memory_space=pltpu.VMEM), hbm],
        out_specs=hbm,
        input_output_aliases={2: 0},
        scratch_shapes=[pltpu.SemaphoreType.DMA],
        name="join",
    )(place, pltpu.with_memory_space_constraint(got, pltpu.VMEM), part)


def fetch(piece, dy, dx):
    pairs = [
        (SIDE * ((y + dy + SIDE) % SIDE) + (x + dx) % SIDE, SIDE * y + x)
        for y in range(SIDE)
        for x in range(SIDE)
    ]
    return lax.ppermute(piece, "fsdp", pairs)


def per_device(queries, keys, values, out_weight, sessions):
    core = lax.axis_index("ctx") % 2
    swap = [(i, i ^ 1) for i in range(lax.axis_size("ctx"))]
    bounds = jnp.stack([jnp.sum(sessions[0] < 1), jnp.sum(sessions[0] < 2)]).astype(jnp.int32)
    place = lax.axis_index("fsdp")
    place = jnp.stack([place // SIDE, place % SIDE, core]).astype(jnp.int32)

    packed = lax.all_to_all(pack(queries, keys, values), "ctx", 0, 0, tiled=True)

    half = out_weight.shape[1] // 2
    first = lax.dynamic_slice_in_dim(out_weight, core * half, half // 2, 1)
    second = lax.dynamic_slice_in_dim(out_weight, core * half + half // 2, half // 2, 1)
    first = jnp.stack([first] + [fetch(first, 0, step) for step in NEAR[1:]])
    second = jnp.stack([second] + [fetch(second, step, 0) for step in NEAR[1:]])
    packed, _, _ = lax.optimization_barrier((packed, first, second))
    passed = [
        fetch(first[:2], 1, 0),
        fetch(first[2:], -1, 0),
        fetch(second[:2], 0, 1),
        fetch(second[2:], 0, -1),
    ]
    beside = [
        fetch(first[2:], 1, 0),
        fetch(first[:2], -1, 0),
        fetch(second[2:], 0, 1),
        fetch(second[:2], 0, -1),
    ]
    packed, *_ = lax.optimization_barrier((packed, *passed))
    far = [
        fetch(passed[0], 1, 0),
        fetch(passed[1], -1, 0),
        fetch(passed[2], 0, 1),
        fetch(passed[3], 0, -1),
    ]
    attended = head_attention(bounds, packed)
    attended, *_ = lax.optimization_barrier((attended, *beside))
    steps = [1, -1, 1, -1, 2, 2]
    lists = [NEAR[:2], NEAR[2:], NEAR[2:], NEAR[:2], NEAR[:2], NEAR[2:]]
    offsets = (
        [[(0, dx) for dx in NEAR]] + [[(dy, dx) for dx in near] for dy, near in zip(steps, lists)],
        [[(dy, 0) for dy in NEAR]] + [[(dy, dx) for dy in near] for dx, near in zip(steps, lists)],
    )
    pieces = [first, *passed[:2], *beside[:2], *far[:2], second, *passed[2:], *beside[2:], *far[2:]]

    mine = lax.all_to_all(attended, "ctx", 0, 0, tiled=True)
    theirs = lax.ppermute(mine, "ctx", swap)
    part, sent = project(place, mine, theirs, pieces, offsets)
    got = lax.ppermute(sent, "ctx", swap)
    return join(place, got, part)


def solution(mesh):
    return jax.shard_map(
        per_device,
        mesh=mesh,
        in_specs=(
            P(("fsdp", "ctx"), None),
            P(("fsdp", "ctx"), None),
            P(("fsdp", "ctx"), None),
            P("fsdp", None),
            P("fsdp", None),
        ),
        out_specs=P(("fsdp", "ctx"), None),
        check_vma=False,
    )
```

```python
import math

import jax
import jax.numpy as jnp
from jax import lax
from jax.experimental import pallas as pl
from jax.experimental.pallas import tpu as pltpu
from jax.sharding import PartitionSpec as P

HDIM = 128
TILE = 512
CHAIN = 256
MASKED = -1e30
SIDE = 4
NEAR = (0, 1, 3, 2)
STRIP = 512


def attention_kernel(bounds_ref, packed_ref, out_ref, vt_ref):
    blocks, _, rows, _ = packed_ref.shape
    slab = blocks * rows
    first, second = bounds_ref[0], bounds_ref[1]
    factor = math.log2(math.e) / math.sqrt(HDIM)
    chains = TILE // CHAIN

    def start_of(position):
        return jnp.where(position >= second, second, jnp.where(position >= first, first, 0))

    def tokens(index, start, count):
        return packed_ref[pl.ds(start // rows, count // rows), index].reshape(count, HDIM)

    for block in range(blocks):
        vt_ref[block] = jnp.transpose(packed_ref[block, 2])

    def values_t(start, count):
        part = vt_ref[pl.ds(start // rows, count // rows)]
        return jnp.concatenate([part[i] for i in range(count // rows)], axis=1)

    def attend(state, query, keys, v_t, mask):
        scores = lax.dot_general(keys, query, (((1,), (1,)), ((), ())), preferred_element_type=jnp.float32)
        if mask is not None:
            scores = jnp.where(mask, scores, MASKED)
        top = jnp.max(scores, axis=0, keepdims=True)
        if state is not None:
            top = jnp.maximum(state[0], top)
        weights = jnp.exp2((scores - top) * factor)
        total = jnp.sum(weights, axis=0, keepdims=True)
        accum = jnp.dot(v_t, weights.astype(jnp.bfloat16), preferred_element_type=jnp.float32)
        if state is not None:
            rescale = jnp.exp2((state[0] - top) * factor)
            total = total + state[1] * rescale
            accum = accum + state[2] * rescale
        return top, total, accum

    for tile in range(slab // TILE):
        base = tile * TILE
        queries, positions, starts, states = [], [], [], []
        for chain in range(chains):
            at = base + chain * CHAIN
            queries.append(tokens(0, at, CHAIN))
            position = at + lax.broadcasted_iota(jnp.int32, (1, CHAIN), 1)
            starts.append(start_of(position))
            count = (chain + 1) * CHAIN
            key_pos = base + lax.broadcasted_iota(jnp.int32, (count, 1), 0)
            mask = (key_pos <= position) & (key_pos >= starts[-1])
            states.append(attend(None, queries[-1], tokens(1, base, count), values_t(base, count), mask))
        if tile:
            low = start_of(jnp.int32(base)) // TILE
            full = jnp.minimum((start_of(jnp.int32(base + TILE - 1)) + TILE - 1) // TILE, tile)

            def step(masked, j, states):
                start = pl.multiple_of(j * TILE, TILE)
                keys, v_t = tokens(1, start, TILE), values_t(start, TILE)
                out = []
                for chain in range(chains):
                    mask = None
                    if masked:
                        mask = start + lax.broadcasted_iota(jnp.int32, (TILE, 1), 0) >= starts[chain]
                    out.append(attend(states[chain], queries[chain], keys, v_t, mask))
                return tuple(out)

            states = lax.fori_loop(full, tile, lambda j, s: step(False, j, s), tuple(states))
            states = lax.fori_loop(low, full, lambda j, s: step(True, j, s), states)
        for chain in range(chains):
            _, total, accum = states[chain]
            finished = jnp.transpose((accum / total).astype(jnp.bfloat16))
            at = (base + chain * CHAIN) // rows
            out_ref[at:at + CHAIN // rows] = finished.reshape(CHAIN // rows, rows, HDIM)


def pack_kernel(queries_ref, keys_ref, values_ref, out_ref):
    for index, ref in enumerate((queries_ref, keys_ref, values_ref)):
        for head in range(out_ref.shape[0]):
            out_ref[head, index] = ref[:, head * HDIM:(head + 1) * HDIM]


def pack(queries, keys, values):
    rows, width = queries.shape
    heads = width // HDIM
    half = pl.BlockSpec((rows, width // 2), lambda i: (0, i))
    return pl.pallas_call(
        pack_kernel,
        out_shape=jax.ShapeDtypeStruct((heads, 3, rows, HDIM), queries.dtype),
        grid=(2,),
        in_specs=[half] * 3,
        out_specs=pl.BlockSpec((heads // 2, 3, rows, HDIM), lambda i: (i, 0, 0, 0)),
        name="pack",
    )(queries, keys, values)


def head_attention(bounds, packed):
    blocks, _, rows, _ = packed.shape
    vmem = pl.BlockSpec(memory_space=pltpu.VMEM)
    return pl.pallas_call(
        attention_kernel,
        out_shape=jax.ShapeDtypeStruct((blocks, rows, HDIM), jnp.bfloat16),
        in_specs=[pl.BlockSpec(memory_space=pltpu.SMEM), vmem],
        out_specs=vmem,
        scratch_shapes=[pltpu.VMEM((blocks, HDIM, rows), jnp.bfloat16)],
        compiler_params=pltpu.CompilerParams(vmem_limit_bytes=16 << 20),
        name="head_attention",
    )(bounds, packed)


def projection_kernel(place_ref, mine_ref, theirs_ref, *rest):
    pieces = rest[:SIDE]
    out_ref, sent_ref, kept_ref, left_ref, weight_ref, weight_semaphores, semaphores = rest[SIDE:]
    columns = pieces[0].shape[2]
    rows = mine_ref.shape[1]
    depth = SIDE * HDIM
    loads = []
    for strip in range(columns // STRIP):
        for i, piece in enumerate(pieces):
            source = piece.at[:, :, strip * STRIP:(strip + 1) * STRIP]
            loads.append(
                pltpu.make_async_copy(source, weight_ref.at[strip, i], weight_semaphores.at[strip, i])
            )
            loads[-1].start()
    y, x, core = place_ref[0], place_ref[1], place_ref[2]
    for i, far in enumerate(NEAR):
        for j, near in enumerate(NEAR):
            dy = jnp.where(core == 0, far, near)
            dx = jnp.where(core == 0, near, far)
            head = ((y + dy) % SIDE) * SIDE + (x + dx) % SIDE
            at = slice(i * depth + j * HDIM, i * depth + (j + 1) * HDIM)
            left_ref[:rows, at] = mine_ref[head]
            left_ref[rows:, at] = theirs_ref[head]
    copies = []
    for strip in range(columns // STRIP):
        at = slice(strip * STRIP, (strip + 1) * STRIP)
        for load in loads[strip * SIDE:(strip + 1) * SIDE]:
            load.wait()
        result = jnp.dot(
            left_ref[...],
            weight_ref[strip].reshape(SIDE * depth, STRIP),
            preferred_element_type=jnp.float32,
        ).astype(jnp.bfloat16)
        sent_ref[:, at] = result[rows:]
        kept_ref[strip] = result[:rows]
        target = pl.multiple_of(core * columns + strip * STRIP, STRIP)
        copies.append(
            pltpu.make_async_copy(
                kept_ref.at[strip], out_ref.at[:, pl.ds(target, STRIP)], semaphores.at[strip]
            )
        )
        copies[-1].start()
    for copy in copies:
        copy.wait()


def project(place, mine, theirs, pieces):
    heads, rows, _ = mine.shape
    columns = pieces[0].shape[2]
    vmem = pl.BlockSpec(memory_space=pltpu.VMEM)
    hbm = pl.BlockSpec(memory_space=pltpu.HBM)
    pieces = [pltpu.with_memory_space_constraint(piece, pltpu.HBM) for piece in pieces]
    return pl.pallas_call(
        projection_kernel,
        out_shape=(
            jax.ShapeDtypeStruct((rows, 2 * columns), jnp.bfloat16),
            jax.ShapeDtypeStruct((rows, columns), jnp.bfloat16),
        ),
        in_specs=[pl.BlockSpec(memory_space=pltpu.SMEM), vmem, vmem] + [hbm] * SIDE,
        out_specs=(hbm, vmem),
        scratch_shapes=[
            pltpu.VMEM((columns // STRIP, rows, STRIP), jnp.bfloat16),
            pltpu.VMEM((2 * rows, heads * HDIM), jnp.bfloat16),
            pltpu.VMEM((columns // STRIP, SIDE, SIDE, HDIM, STRIP), jnp.bfloat16),
            pltpu.SemaphoreType.DMA((columns // STRIP, SIDE)),
            pltpu.SemaphoreType.DMA((columns // STRIP,)),
        ],
        compiler_params=pltpu.CompilerParams(vmem_limit_bytes=20 << 20),
        name="project",
    )(place, mine, theirs, *pieces)


def join_kernel(place_ref, got_ref, part_ref, out_ref, semaphore):
    half = got_ref.shape[1]
    other = pl.multiple_of((1 - place_ref[2]) * half, half)
    copy = pltpu.make_async_copy(got_ref, out_ref.at[:, pl.ds(other, half)], semaphore)
    copy.start()
    copy.wait()


def join(place, got, part):
    hbm = pl.BlockSpec(memory_space=pltpu.HBM)
    return pl.pallas_call(
        join_kernel,
        out_shape=jax.ShapeDtypeStruct(part.shape, part.dtype),
        in_specs=[pl.BlockSpec(memory_space=pltpu.SMEM), pl.BlockSpec(memory_space=pltpu.VMEM), hbm],
        out_specs=hbm,
        input_output_aliases={2: 0},
        scratch_shapes=[pltpu.SemaphoreType.DMA],
        name="join",
    )(place, pltpu.with_memory_space_constraint(got, pltpu.VMEM), part)


def fetch(piece, step, near):
    count = lax.axis_size("ctx")
    pairs = []
    for y in range(SIDE):
        for x in range(SIDE):
            for place in range(count):
                along_x = (place % 2 == 0) == near
                source_y = y if along_x else (y + step) % SIDE
                source_x = (x + step) % SIDE if along_x else x
                pairs.append(
                    ((SIDE * source_y + source_x) * count + place, (SIDE * y + x) * count + place)
                )
    return lax.ppermute(piece, ("fsdp", "ctx"), pairs)


def per_device(queries, keys, values, out_weight, sessions):
    core = lax.axis_index("ctx") % 2
    swap = [(i, i ^ 1) for i in range(lax.axis_size("ctx"))]
    bounds = jnp.stack([jnp.sum(sessions[0] < 1), jnp.sum(sessions[0] < 2)]).astype(jnp.int32)
    place = lax.axis_index("fsdp")
    place = jnp.stack([place // SIDE, place % SIDE, core]).astype(jnp.int32)

    packed = lax.all_to_all(pack(queries, keys, values), "ctx", 0, 0, tiled=True)

    half = out_weight.shape[1] // 2
    own = lax.dynamic_slice_in_dim(out_weight, core * half, half, 1)
    line = jnp.stack([own] + [fetch(own, step, True) for step in NEAR[1:]])
    packed, _ = lax.optimization_barrier((packed, line))
    pieces = [line] + [fetch(line, step, False) for step in NEAR[1:]]

    attended = head_attention(bounds, packed)
    mine = lax.all_to_all(attended, "ctx", 0, 0, tiled=True)
    theirs = lax.ppermute(mine, "ctx", swap)
    part, sent = project(place, mine, theirs, pieces)
    got = lax.ppermute(sent, "ctx", swap)
    return join(place, got, part)


def solution(mesh):
    return jax.shard_map(
        per_device,
        mesh=mesh,
        in_specs=(
            P(("fsdp", "ctx"), None),
            P(("fsdp", "ctx"), None),
            P(("fsdp", "ctx"), None),
            P("fsdp", None),
            P("fsdp", None),
        ),
        out_specs=P(("fsdp", "ctx"), None),
        check_vma=False,
    )
```

```python
import functools
import math

import jax
import jax.numpy as jnp
from jax import lax
from jax.experimental import pallas as pl
from jax.experimental.pallas import tpu as pltpu
from jax.sharding import PartitionSpec as P

HDIM = 128
TILE = 512
CHAIN = 512
MASKED = -1e30
SIDE = 4
STRIP = 512


def attention_kernel(bounds_ref, packed_ref, out_ref, vt_ref):
    blocks, _, rows, _ = packed_ref.shape
    slab = blocks * rows
    first, second = bounds_ref[0], bounds_ref[1]
    factor = math.log2(math.e) / math.sqrt(HDIM)
    chains = TILE // CHAIN

    def start_of(position):
        return jnp.where(position >= second, second, jnp.where(position >= first, first, 0))

    def tokens(index, start, count):
        return packed_ref[pl.ds(start // rows, count // rows), index].reshape(count, HDIM)

    for block in range(blocks):
        vt_ref[block] = jnp.transpose(packed_ref[block, 2])

    def values_t(start, count):
        part = vt_ref[pl.ds(start // rows, count // rows)]
        return jnp.concatenate([part[i] for i in range(count // rows)], axis=1)

    def attend(state, query, keys, v_t, mask):
        scores = lax.dot_general(keys, query, (((1,), (1,)), ((), ())), preferred_element_type=jnp.float32)
        if mask is not None:
            scores = jnp.where(mask, scores, MASKED)
        top = jnp.max(scores, axis=0, keepdims=True)
        if state is not None:
            top = jnp.maximum(state[0], top)
        weights = jnp.exp2((scores - top) * factor)
        total = jnp.sum(weights, axis=0, keepdims=True)
        accum = jnp.dot(v_t, weights.astype(jnp.bfloat16), preferred_element_type=jnp.float32)
        if state is not None:
            rescale = jnp.exp2((state[0] - top) * factor)
            total = total + state[1] * rescale
            accum = accum + state[2] * rescale
        return top, total, accum

    for tile in range(slab // TILE):
        base = tile * TILE
        queries, positions, starts, states = [], [], [], []
        for chain in range(chains):
            at = base + chain * CHAIN
            queries.append(tokens(0, at, CHAIN))
            position = at + lax.broadcasted_iota(jnp.int32, (1, CHAIN), 1)
            starts.append(start_of(position))
            count = (chain + 1) * CHAIN
            key_pos = base + lax.broadcasted_iota(jnp.int32, (count, 1), 0)
            mask = (key_pos <= position) & (key_pos >= starts[-1])
            states.append(attend(None, queries[-1], tokens(1, base, count), values_t(base, count), mask))
        if tile:
            low = start_of(jnp.int32(base)) // TILE
            full = jnp.minimum((start_of(jnp.int32(base + TILE - 1)) + TILE - 1) // TILE, tile)

            def step(masked, j, states):
                start = pl.multiple_of(j * TILE, TILE)
                keys, v_t = tokens(1, start, TILE), values_t(start, TILE)
                out = []
                for chain in range(chains):
                    mask = None
                    if masked:
                        mask = start + lax.broadcasted_iota(jnp.int32, (TILE, 1), 0) >= starts[chain]
                    out.append(attend(states[chain], queries[chain], keys, v_t, mask))
                return tuple(out)

            states = lax.fori_loop(full, tile, lambda j, s: step(False, j, s), tuple(states))
            states = lax.fori_loop(low, full, lambda j, s: step(True, j, s), states)
        for chain in range(chains):
            _, total, accum = states[chain]
            finished = jnp.transpose((accum / total).astype(jnp.bfloat16))
            at = (base + chain * CHAIN) // rows
            out_ref[at:at + CHAIN // rows] = finished.reshape(CHAIN // rows, rows, HDIM)


def pack_kernel(queries_ref, keys_ref, values_ref, out_ref):
    for index, ref in enumerate((queries_ref, keys_ref, values_ref)):
        for head in range(out_ref.shape[0]):
            out_ref[head, index] = ref[:, head * HDIM:(head + 1) * HDIM]


def pack(queries, keys, values):
    rows, width = queries.shape
    heads = width // HDIM
    half = pl.BlockSpec((rows, width // 2), lambda i: (0, i))
    return pl.pallas_call(
        pack_kernel,
        out_shape=jax.ShapeDtypeStruct((heads, 3, rows, HDIM), queries.dtype),
        grid=(2,),
        in_specs=[half] * 3,
        out_specs=pl.BlockSpec((heads // 2, 3, rows, HDIM), lambda i: (i, 0, 0, 0)),
        name="pack",
    )(queries, keys, values)


def head_attention(bounds, packed):
    blocks, _, rows, _ = packed.shape
    vmem = pl.BlockSpec(memory_space=pltpu.VMEM)
    return pl.pallas_call(
        attention_kernel,
        out_shape=jax.ShapeDtypeStruct((blocks, rows, HDIM), jnp.bfloat16),
        in_specs=[pl.BlockSpec(memory_space=pltpu.SMEM), vmem],
        out_specs=vmem,
        scratch_shapes=[pltpu.VMEM((blocks, HDIM, rows), jnp.bfloat16)],
        compiler_params=pltpu.CompilerParams(vmem_limit_bytes=16 << 20),
        name="head_attention",
    )(bounds, packed)


def projection_kernel(places, place_ref, mine_ref, theirs_ref, *rest):
    pieces = rest[:-7]
    out_ref, sent_ref, kept_ref, left_ref, weight_ref, weight_semaphores, semaphores = rest[-7:]
    columns = sent_ref.shape[1]
    rows = mine_ref.shape[1]
    loads = []
    for strip in range(columns // STRIP):
        at = 0
        for i, piece in enumerate(pieces):
            count = piece.shape[0]
            source = piece.at[:, :, strip * STRIP:(strip + 1) * STRIP]
            target = weight_ref.at[strip, pl.ds(at, count)]
            loads.append(pltpu.make_async_copy(source, target, weight_semaphores.at[strip, i]))
            loads[-1].start()
            at += count
    y, x, core = place_ref[0], place_ref[1], place_ref[2]
    for i, (far, near) in enumerate(places):
        dy = jnp.where(core == 0, far, near)
        dx = jnp.where(core == 0, near, far)
        head = ((y + dy) % SIDE) * SIDE + (x + dx) % SIDE
        left_ref[:rows, i * HDIM:(i + 1) * HDIM] = mine_ref[head]
        left_ref[rows:, i * HDIM:(i + 1) * HDIM] = theirs_ref[head]
    copies = []
    for strip in range(columns // STRIP):
        at = slice(strip * STRIP, (strip + 1) * STRIP)
        for load in loads[strip * len(pieces):(strip + 1) * len(pieces)]:
            load.wait()
        result = jnp.dot(
            left_ref[...],
            weight_ref[strip].reshape(len(places) * HDIM, STRIP),
            preferred_element_type=jnp.float32,
        ).astype(jnp.bfloat16)
        sent_ref[:, at] = result[rows:]
        kept_ref[strip] = result[:rows]
        target = pl.multiple_of(core * columns + strip * STRIP, STRIP)
        copies.append(
            pltpu.make_async_copy(
                kept_ref.at[strip], out_ref.at[:, pl.ds(target, STRIP)], semaphores.at[strip]
            )
        )
        copies[-1].start()
    for copy in copies:
        copy.wait()


def project(place, mine, theirs, pieces, places):
    heads, rows, _ = mine.shape
    columns = pieces[0].shape[2]
    strips = columns // STRIP
    vmem = pl.BlockSpec(memory_space=pltpu.VMEM)
    hbm = pl.BlockSpec(memory_space=pltpu.HBM)
    pieces = [pltpu.with_memory_space_constraint(piece, pltpu.HBM) for piece in pieces]
    return pl.pallas_call(
        functools.partial(projection_kernel, places),
        out_shape=(
            jax.ShapeDtypeStruct((rows, 2 * columns), jnp.bfloat16),
            jax.ShapeDtypeStruct((rows, columns), jnp.bfloat16),
        ),
        in_specs=[pl.BlockSpec(memory_space=pltpu.SMEM), vmem, vmem] + [hbm] * len(pieces),
        out_specs=(hbm, vmem),
        scratch_shapes=[
            pltpu.VMEM((strips, rows, STRIP), jnp.bfloat16),
            pltpu.VMEM((2 * rows, heads * HDIM), jnp.bfloat16),
            pltpu.VMEM((strips, heads, HDIM, STRIP), jnp.bfloat16),
            pltpu.SemaphoreType.DMA((strips, len(pieces))),
            pltpu.SemaphoreType.DMA((strips,)),
        ],
        compiler_params=pltpu.CompilerParams(vmem_limit_bytes=20 << 20),
        name="project",
    )(place, mine, theirs, *pieces)


def fetch(piece, step, near):
    count = lax.axis_size("ctx")
    pairs = []
    for y in range(SIDE):
        for x in range(SIDE):
            for place in range(count):
                along_x = (place % 2 == 0) == near
                source_y = y if along_x else (y + step) % SIDE
                source_x = (x + step) % SIDE if along_x else x
                pairs.append(
                    ((SIDE * source_y + source_x) * count + place, (SIDE * y + x) * count + place)
                )
    return lax.ppermute(piece, ("fsdp", "ctx"), pairs)


def per_device(queries, keys, values, out_weight, sessions):
    core = lax.axis_index("ctx") % 2
    swap = [(i, i ^ 1) for i in range(lax.axis_size("ctx"))]
    bounds = jnp.stack([jnp.sum(sessions[0] < 1), jnp.sum(sessions[0] < 2)]).astype(jnp.int32)
    place = lax.axis_index("fsdp")
    place = jnp.stack([place // SIDE, place % SIDE, core]).astype(jnp.int32)

    packed = lax.all_to_all(pack(queries, keys, values), "ctx", 0, 0, tiled=True)

    half = out_weight.shape[1] // 2
    own = lax.dynamic_slice_in_dim(out_weight, core * half, half, 1)
    low = jnp.stack([own, fetch(own, 1, True)])
    high = jnp.stack([fetch(own, -1, True), fetch(own, 2, True)])
    after = fetch(low, 1, False)
    before = fetch(high, -1, False)
    right = fetch(jnp.concatenate([high, after]), 1, False)
    left = fetch(jnp.concatenate([low, before]), -1, False)
    pieces = [low, high, after, before, right, left]
    places = [(0, 0), (0, 1), (0, 3), (0, 2), (1, 0), (1, 1), (3, 3), (3, 2)]
    places += [(1, 3), (1, 2), (2, 0), (2, 1), (3, 0), (3, 1), (2, 3), (2, 2)]
    packed, *_ = lax.optimization_barrier((packed, after, before))

    attended = head_attention(bounds, packed)
    mine = lax.all_to_all(attended, "ctx", 0, 0, tiled=True)
    theirs = lax.ppermute(mine, "ctx", swap)
    part, sent = project(place, mine, theirs, pieces, places)
    got = lax.ppermute(sent, "ctx", swap)
    return lax.dynamic_update_slice(part, got, (0, (1 - core) * half))


def solution(mesh):
    return jax.shard_map(
        per_device,
        mesh=mesh,
        in_specs=(
            P(("fsdp", "ctx"), None),
            P(("fsdp", "ctx"), None),
            P(("fsdp", "ctx"), None),
            P("fsdp", None),
            P("fsdp", None),
        ),
        out_specs=P(("fsdp", "ctx"), None),
        check_vma=False,
    )
```

```python
import functools
import math

import jax
import jax.numpy as jnp
from jax import lax
from jax.experimental import pallas as pl
from jax.experimental.pallas import tpu as pltpu
from jax.sharding import PartitionSpec as P

HDIM = 128
TILE = 512
CHAIN = 512
MASKED = -1e30
SIDE = 4
NEAR = (0, 1, 3, 2)
STRIP = 512


def attention_kernel(bounds_ref, packed_ref, out_ref, vt_ref):
    blocks, _, rows, _ = packed_ref.shape
    slab = blocks * rows
    first, second = bounds_ref[0], bounds_ref[1]
    factor = math.log2(math.e) / math.sqrt(HDIM)
    chains = TILE // CHAIN

    def start_of(position):
        return jnp.where(position >= second, second, jnp.where(position >= first, first, 0))

    def tokens(index, start, count):
        return packed_ref[pl.ds(start // rows, count // rows), index].reshape(count, HDIM)

    for block in range(blocks):
        vt_ref[block] = jnp.transpose(packed_ref[block, 2])

    def values_t(start, count):
        part = vt_ref[pl.ds(start // rows, count // rows)]
        return jnp.concatenate([part[i] for i in range(count // rows)], axis=1)

    def attend(state, query, keys, v_t, mask):
        scores = lax.dot_general(keys, query, (((1,), (1,)), ((), ())), preferred_element_type=jnp.float32)
        if mask is not None:
            scores = jnp.where(mask, scores, MASKED)
        top = jnp.max(scores, axis=0, keepdims=True)
        if state is not None:
            top = jnp.maximum(state[0], top)
        weights = jnp.exp2((scores - top) * factor)
        total = jnp.sum(weights, axis=0, keepdims=True)
        accum = jnp.dot(v_t, weights.astype(jnp.bfloat16), preferred_element_type=jnp.float32)
        if state is not None:
            rescale = jnp.exp2((state[0] - top) * factor)
            total = total + state[1] * rescale
            accum = accum + state[2] * rescale
        return top, total, accum

    for tile in range(slab // TILE):
        base = tile * TILE
        queries, positions, starts, states = [], [], [], []
        for chain in range(chains):
            at = base + chain * CHAIN
            queries.append(tokens(0, at, CHAIN))
            position = at + lax.broadcasted_iota(jnp.int32, (1, CHAIN), 1)
            starts.append(start_of(position))
            count = (chain + 1) * CHAIN
            key_pos = base + lax.broadcasted_iota(jnp.int32, (count, 1), 0)
            mask = (key_pos <= position) & (key_pos >= starts[-1])
            states.append(attend(None, queries[-1], tokens(1, base, count), values_t(base, count), mask))
        if tile:
            low = start_of(jnp.int32(base)) // TILE
            full = jnp.minimum((start_of(jnp.int32(base + TILE - 1)) + TILE - 1) // TILE, tile)

            def step(masked, j, states):
                start = pl.multiple_of(j * TILE, TILE)
                keys, v_t = tokens(1, start, TILE), values_t(start, TILE)
                out = []
                for chain in range(chains):
                    mask = None
                    if masked:
                        mask = start + lax.broadcasted_iota(jnp.int32, (TILE, 1), 0) >= starts[chain]
                    out.append(attend(states[chain], queries[chain], keys, v_t, mask))
                return tuple(out)

            states = lax.fori_loop(full, tile, lambda j, s: step(False, j, s), tuple(states))
            states = lax.fori_loop(low, full, lambda j, s: step(True, j, s), states)
        for chain in range(chains):
            _, total, accum = states[chain]
            finished = jnp.transpose((accum / total).astype(jnp.bfloat16))
            at = (base + chain * CHAIN) // rows
            out_ref[at:at + CHAIN // rows] = finished.reshape(CHAIN // rows, rows, HDIM)


def pack_kernel(queries_ref, keys_ref, values_ref, out_ref):
    for index, ref in enumerate((queries_ref, keys_ref, values_ref)):
        for head in range(out_ref.shape[0]):
            out_ref[head, index] = ref[:, head * HDIM:(head + 1) * HDIM]


def pack(queries, keys, values):
    rows, width = queries.shape
    heads = width // HDIM
    half = pl.BlockSpec((rows, width // 2), lambda i: (0, i))
    return pl.pallas_call(
        pack_kernel,
        out_shape=jax.ShapeDtypeStruct((heads, 3, rows, HDIM), queries.dtype),
        grid=(2,),
        in_specs=[half] * 3,
        out_specs=pl.BlockSpec((heads // 2, 3, rows, HDIM), lambda i: (i, 0, 0, 0)),
        name="pack",
    )(queries, keys, values)


def head_attention(bounds, packed):
    blocks, _, rows, _ = packed.shape
    vmem = pl.BlockSpec(memory_space=pltpu.VMEM)
    return pl.pallas_call(
        attention_kernel,
        out_shape=jax.ShapeDtypeStruct((blocks, rows, HDIM), jnp.bfloat16),
        in_specs=[pl.BlockSpec(memory_space=pltpu.SMEM), vmem],
        out_specs=vmem,
        scratch_shapes=[pltpu.VMEM((blocks, HDIM, rows), jnp.bfloat16)],
        compiler_params=pltpu.CompilerParams(vmem_limit_bytes=16 << 20),
        name="head_attention",
    )(bounds, packed)


def projection_kernel(places, place_ref, mine_ref, theirs_ref, *rest):
    pieces = rest[:-7]
    out_ref, sent_ref, kept_ref, left_ref, weight_ref, weight_semaphores, semaphores = rest[-7:]
    columns = sent_ref.shape[1]
    rows = mine_ref.shape[1]
    loads = []
    for strip in range(columns // STRIP):
        at = 0
        for i, piece in enumerate(pieces):
            count = piece.shape[0]
            source = piece.at[:, :, strip * STRIP:(strip + 1) * STRIP]
            target = weight_ref.at[strip, pl.ds(at, count)]
            loads.append(pltpu.make_async_copy(source, target, weight_semaphores.at[strip, i]))
            loads[-1].start()
            at += count
    y, x, core = place_ref[0], place_ref[1], place_ref[2]
    for i, (far, near) in enumerate(places):
        dy = jnp.where(core == 0, far, near)
        dx = jnp.where(core == 0, near, far)
        head = ((y + dy) % SIDE) * SIDE + (x + dx) % SIDE
        left_ref[:rows, i * HDIM:(i + 1) * HDIM] = mine_ref[head]
        left_ref[rows:, i * HDIM:(i + 1) * HDIM] = theirs_ref[head]
    copies = []
    for strip in range(columns // STRIP):
        at = slice(strip * STRIP, (strip + 1) * STRIP)
        for load in loads[strip * len(pieces):(strip + 1) * len(pieces)]:
            load.wait()
        result = jnp.dot(
            left_ref[...],
            weight_ref[strip].reshape(len(places) * HDIM, STRIP),
            preferred_element_type=jnp.float32,
        ).astype(jnp.bfloat16)
        sent_ref[:, at] = result[rows:]
        kept_ref[strip] = result[:rows]
        target = pl.multiple_of(core * columns + strip * STRIP, STRIP)
        copies.append(
            pltpu.make_async_copy(
                kept_ref.at[strip], out_ref.at[:, pl.ds(target, STRIP)], semaphores.at[strip]
            )
        )
        copies[-1].start()
    for copy in copies:
        copy.wait()


def project(place, mine, theirs, pieces, places):
    heads, rows, _ = mine.shape
    columns = pieces[0].shape[2]
    strips = columns // STRIP
    vmem = pl.BlockSpec(memory_space=pltpu.VMEM)
    hbm = pl.BlockSpec(memory_space=pltpu.HBM)
    pieces = [pltpu.with_memory_space_constraint(piece, pltpu.HBM) for piece in pieces]
    return pl.pallas_call(
        functools.partial(projection_kernel, places),
        out_shape=(
            jax.ShapeDtypeStruct((rows, 2 * columns), jnp.bfloat16),
            jax.ShapeDtypeStruct((rows, columns), jnp.bfloat16),
        ),
        in_specs=[pl.BlockSpec(memory_space=pltpu.SMEM), vmem, vmem] + [hbm] * len(pieces),
        out_specs=(hbm, vmem),
        scratch_shapes=[
            pltpu.VMEM((strips, rows, STRIP), jnp.bfloat16),
            pltpu.VMEM((2 * rows, heads * HDIM), jnp.bfloat16),
            pltpu.VMEM((strips, heads, HDIM, STRIP), jnp.bfloat16),
            pltpu.SemaphoreType.DMA((strips, len(pieces))),
            pltpu.SemaphoreType.DMA((strips,)),
        ],
        compiler_params=pltpu.CompilerParams(vmem_limit_bytes=20 << 20),
        name="project",
    )(place, mine, theirs, *pieces)


def fetch(piece, step, near):
    count = lax.axis_size("ctx")
    pairs = []
    for y in range(SIDE):
        for x in range(SIDE):
            for place in range(count):
                along_x = (place % 2 == 0) == near
                source_y = y if along_x else (y + step) % SIDE
                source_x = (x + step) % SIDE if along_x else x
                pairs.append(
                    ((SIDE * source_y + source_x) * count + place, (SIDE * y + x) * count + place)
                )
    return lax.ppermute(piece, ("fsdp", "ctx"), pairs)


def per_device(queries, keys, values, out_weight, sessions):
    core = lax.axis_index("ctx") % 2
    swap = [(i, i ^ 1) for i in range(lax.axis_size("ctx"))]
    bounds = jnp.stack([jnp.sum(sessions[0] < 1), jnp.sum(sessions[0] < 2)]).astype(jnp.int32)
    place = lax.axis_index("fsdp")
    place = jnp.stack([place // SIDE, place % SIDE, core]).astype(jnp.int32)

    packed = lax.all_to_all(pack(queries, keys, values), "ctx", 0, 0, tiled=True)

    half = out_weight.shape[1] // 2
    own = lax.dynamic_slice_in_dim(out_weight, core * half, half, 1)
    line = jnp.stack([own] + [fetch(own, step, True) for step in NEAR[1:]])
    packed, _ = lax.optimization_barrier((packed, line))
    pieces = [line] + [fetch(line, step, False) for step in NEAR[1:]]
    places = [(far, near) for far in NEAR for near in NEAR]
    attended = head_attention(bounds, packed)
    mine = lax.all_to_all(attended, "ctx", 0, 0, tiled=True)
    theirs = lax.ppermute(mine, "ctx", swap)
    part, sent = project(place, mine, theirs, pieces, places)
    got = lax.ppermute(sent, "ctx", swap)
    return lax.dynamic_update_slice(part, got, (0, (1 - core) * half))


def solution(mesh):
    return jax.shard_map(
        per_device,
        mesh=mesh,
        in_specs=(
            P(("fsdp", "ctx"), None),
            P(("fsdp", "ctx"), None),
            P(("fsdp", "ctx"), None),
            P("fsdp", None),
            P("fsdp", None),
        ),
        out_specs=P(("fsdp", "ctx"), None),
        check_vma=False,
    )
```

```python
import functools
import math

import jax
import jax.numpy as jnp
from jax import lax
from jax.experimental import pallas as pl
from jax.experimental.pallas import tpu as pltpu
from jax.sharding import PartitionSpec as P

HDIM = 128
TILE = 512
HALF = TILE // 2
MASKED = -1e30
SIDE = 4
NEAR = (0, 1, 3, 2)
STRIP = 512


def attention_kernel(bounds_ref, packed_ref, out_ref, vt_ref):
    blocks, _, rows, _ = packed_ref.shape
    slab = blocks * rows
    first, second = bounds_ref[0], bounds_ref[1]
    factor = math.log2(math.e) / math.sqrt(HDIM)

    def start_of(position):
        return jnp.where(position >= second, second, jnp.where(position >= first, first, 0))

    def tokens(index, start, count):
        return packed_ref[pl.ds(start // rows, count // rows), index].reshape(count, HDIM)

    for block in range(blocks):
        vt_ref[block] = jnp.transpose(packed_ref[block, 2])

    def values_t(start, count):
        part = vt_ref[pl.ds(start // rows, count // rows)]
        return jnp.concatenate([part[i] for i in range(count // rows)], axis=1)

    def attend(state, query, keys, v_t, mask):
        scores = lax.dot_general(keys, query, (((1,), (1,)), ((), ())), preferred_element_type=jnp.float32)
        if mask is not None:
            scores = jnp.where(mask, scores, MASKED)
        top = jnp.max(scores, axis=0, keepdims=True)
        if state is not None:
            top = jnp.maximum(state[0], top)
        weights = jnp.exp2((scores - top) * factor)
        total = jnp.sum(weights, axis=0, keepdims=True)
        accum = jnp.dot(v_t, weights.astype(jnp.bfloat16), preferred_element_type=jnp.float32)
        if state is not None:
            rescale = jnp.exp2((state[0] - top) * factor)
            total = total + state[1] * rescale
            accum = accum + state[2] * rescale
        return top, total, accum

    for tile in range(slab // TILE):
        base = tile * TILE
        query = tokens(0, base, TILE)
        position = base + lax.broadcasted_iota(jnp.int32, (1, TILE), 1)
        starts = start_of(position)
        key_pos = base + lax.broadcasted_iota(jnp.int32, (TILE, 1), 0)
        mask = (key_pos <= position) & (key_pos >= starts)
        state = attend(None, query, tokens(1, base, TILE), values_t(base, TILE), mask)
        if tile:
            begin = start_of(jnp.int32(base))
            low = begin // TILE
            full = jnp.minimum((start_of(jnp.int32(base + TILE - 1)) + TILE - 1) // TILE, tile)
            ends = jnp.minimum(
                jnp.where(first > base, first, slab), jnp.where(second > base, second, slab)
            )
            narrow = ends - base <= HALF
            short = jnp.logical_not(narrow) & (low < full) & (begin - low * TILE >= HALF)
            short = short.astype(jnp.int32)

            def masked(state, query, start, count, starts):
                mask = start + lax.broadcasted_iota(jnp.int32, (count, 1), 0) >= starts
                return attend(state, query, tokens(1, start, count), values_t(start, count), mask)

            def whole(j, state):
                start = pl.multiple_of(j * TILE, TILE)
                return attend(state, query, tokens(1, start, TILE), values_t(start, TILE), None)

            def wide(j, state):
                return masked(state, query, pl.multiple_of(j * TILE, TILE), TILE, starts)

            def second_half(_, state):
                return masked(state, query, pl.multiple_of(low * TILE + HALF, HALF), HALF, starts)

            def first_queries(j, state):
                part = tuple(item[:, :HALF] for item in state)
                start = pl.multiple_of(j * TILE, TILE)
                part = masked(part, query[:HALF], start, TILE, starts[:, :HALF])
                return tuple(
                    jnp.concatenate([new, old[:, HALF:]], axis=1) for new, old in zip(part, state)
                )

            state = lax.fori_loop(full, tile, whole, state)
            state = lax.fori_loop(low + short, jnp.where(narrow, low, full), wide, state)
            state = lax.fori_loop(0, short, second_half, state)
            state = lax.fori_loop(low, jnp.where(narrow, full, low), first_queries, state)
        _, total, accum = state
        finished = jnp.transpose((accum / total).astype(jnp.bfloat16))
        out_ref[base // rows:(base + TILE) // rows] = finished.reshape(TILE // rows, rows, HDIM)


def pack_kernel(queries_ref, keys_ref, values_ref, out_ref):
    for index, ref in enumerate((queries_ref, keys_ref, values_ref)):
        for head in range(out_ref.shape[0]):
            out_ref[head, index] = ref[:, head * HDIM:(head + 1) * HDIM]


def pack(queries, keys, values):
    rows, width = queries.shape
    heads = width // HDIM
    half = pl.BlockSpec((rows, width // 2), lambda i: (0, i))
    return pl.pallas_call(
        pack_kernel,
        out_shape=jax.ShapeDtypeStruct((heads, 3, rows, HDIM), queries.dtype),
        grid=(2,),
        in_specs=[half] * 3,
        out_specs=pl.BlockSpec((heads // 2, 3, rows, HDIM), lambda i: (i, 0, 0, 0)),
        name="pack",
    )(queries, keys, values)


def head_attention(bounds, packed):
    blocks, _, rows, _ = packed.shape
    vmem = pl.BlockSpec(memory_space=pltpu.VMEM)
    return pl.pallas_call(
        attention_kernel,
        out_shape=jax.ShapeDtypeStruct((blocks, rows, HDIM), jnp.bfloat16),
        in_specs=[pl.BlockSpec(memory_space=pltpu.SMEM), vmem],
        out_specs=vmem,
        scratch_shapes=[pltpu.VMEM((blocks, HDIM, rows), jnp.bfloat16)],
        compiler_params=pltpu.CompilerParams(vmem_limit_bytes=16 << 20),
        name="head_attention",
    )(bounds, packed)


def projection_kernel(places, place_ref, mine_ref, theirs_ref, *rest):
    pieces = rest[:-7]
    out_ref, sent_ref, kept_ref, left_ref, weight_ref, weight_semaphores, semaphores = rest[-7:]
    columns = sent_ref.shape[1]
    rows = mine_ref.shape[1]
    loads = []
    for strip in range(columns // STRIP):
        at = 0
        for i, piece in enumerate(pieces):
            count = piece.shape[0]
            source = piece.at[:, :, strip * STRIP:(strip + 1) * STRIP]
            target = weight_ref.at[strip, pl.ds(at, count)]
            loads.append(pltpu.make_async_copy(source, target, weight_semaphores.at[strip, i]))
            loads[-1].start()
            at += count
    y, x, core = place_ref[0], place_ref[1], place_ref[2]
    for i, (far, near) in enumerate(places):
        dy = jnp.where(core == 0, far, near)
        dx = jnp.where(core == 0, near, far)
        head = ((y + dy) % SIDE) * SIDE + (x + dx) % SIDE
        left_ref[:rows, i * HDIM:(i + 1) * HDIM] = mine_ref[head]
        left_ref[rows:, i * HDIM:(i + 1) * HDIM] = theirs_ref[head]
    copies = []
    for strip in range(columns // STRIP):
        at = slice(strip * STRIP, (strip + 1) * STRIP)
        for load in loads[strip * len(pieces):(strip + 1) * len(pieces)]:
            load.wait()
        result = jnp.dot(
            left_ref[...],
            weight_ref[strip].reshape(len(places) * HDIM, STRIP),
            preferred_element_type=jnp.float32,
        ).astype(jnp.bfloat16)
        sent_ref[:, at] = result[rows:]
        kept_ref[strip] = result[:rows]
        target = pl.multiple_of(core * columns + strip * STRIP, STRIP)
        copies.append(
            pltpu.make_async_copy(
                kept_ref.at[strip], out_ref.at[:, pl.ds(target, STRIP)], semaphores.at[strip]
            )
        )
        copies[-1].start()
    for copy in copies:
        copy.wait()


def project(place, mine, theirs, pieces, places):
    heads, rows, _ = mine.shape
    columns = pieces[0].shape[2]
    strips = columns // STRIP
    vmem = pl.BlockSpec(memory_space=pltpu.VMEM)
    hbm = pl.BlockSpec(memory_space=pltpu.HBM)
    pieces = [pltpu.with_memory_space_constraint(piece, pltpu.HBM) for piece in pieces]
    return pl.pallas_call(
        functools.partial(projection_kernel, places),
        out_shape=(
            jax.ShapeDtypeStruct((rows, 2 * columns), jnp.bfloat16),
            jax.ShapeDtypeStruct((rows, columns), jnp.bfloat16),
        ),
        in_specs=[pl.BlockSpec(memory_space=pltpu.SMEM), vmem, vmem] + [hbm] * len(pieces),
        out_specs=(hbm, vmem),
        scratch_shapes=[
            pltpu.VMEM((strips, rows, STRIP), jnp.bfloat16),
            pltpu.VMEM((2 * rows, heads * HDIM), jnp.bfloat16),
            pltpu.VMEM((strips, heads, HDIM, STRIP), jnp.bfloat16),
            pltpu.SemaphoreType.DMA((strips, len(pieces))),
            pltpu.SemaphoreType.DMA((strips,)),
        ],
        compiler_params=pltpu.CompilerParams(vmem_limit_bytes=20 << 20),
        name="project",
    )(place, mine, theirs, *pieces)


def fetch(piece, step, near):
    count = lax.axis_size("ctx")
    pairs = []
    for y in range(SIDE):
        for x in range(SIDE):
            for place in range(count):
                along_x = (place % 2 == 0) == near
                source_y = y if along_x else (y + step) % SIDE
                source_x = (x + step) % SIDE if along_x else x
                pairs.append(
                    ((SIDE * source_y + source_x) * count + place, (SIDE * y + x) * count + place)
                )
    return lax.ppermute(piece, ("fsdp", "ctx"), pairs)


def per_device(queries, keys, values, out_weight, sessions):
    core = lax.axis_index("ctx") % 2
    swap = [(i, i ^ 1) for i in range(lax.axis_size("ctx"))]
    bounds = jnp.stack([jnp.sum(sessions[0] < 1), jnp.sum(sessions[0] < 2)]).astype(jnp.int32)
    place = lax.axis_index("fsdp")
    place = jnp.stack([place // SIDE, place % SIDE, core]).astype(jnp.int32)

    packed = lax.all_to_all(pack(queries, keys, values), "ctx", 0, 0, tiled=True)

    half = out_weight.shape[1] // 2
    own = lax.dynamic_slice_in_dim(out_weight, core * half, half, 1)
    own = own[None]
    across = fetch(own, 2, False)
    near = [fetch(own, step, True) for step in (1, 3, 2)]
    line = jnp.concatenate([own] + near)
    near = jnp.concatenate(near)
    packed, *_ = lax.optimization_barrier((packed, line, near))
    pieces = [line, fetch(line, 1, False), fetch(line, 3, False), across, fetch(near, 2, False)]
    places = [(far, step) for far in NEAR for step in NEAR]
    attended = head_attention(bounds, packed)
    attended, _ = lax.optimization_barrier((attended, across))
    mine = lax.all_to_all(attended, "ctx", 0, 0, tiled=True)
    theirs = lax.ppermute(mine, "ctx", swap)
    part, sent = project(place, mine, theirs, pieces, places)
    got = lax.ppermute(sent, "ctx", swap)
    return lax.dynamic_update_slice(part, got, (0, (1 - core) * half))


def solution(mesh):
    return jax.shard_map(
        per_device,
        mesh=mesh,
        in_specs=(
            P(("fsdp", "ctx"), None),
            P(("fsdp", "ctx"), None),
            P(("fsdp", "ctx"), None),
            P("fsdp", None),
            P("fsdp", None),
        ),
        out_specs=P(("fsdp", "ctx"), None),
        check_vma=False,
    )
```

```python
import functools
import math

import jax
import jax.numpy as jnp
from jax import lax
from jax.experimental import pallas as pl
from jax.experimental.pallas import tpu as pltpu
from jax.sharding import PartitionSpec as P

HDIM = 128
TILE = 512
HALF = TILE // 2
MASKED = -1e30
SIDE = 4
NEAR = (0, 1, 3, 2)
STRIP = 512


def attention_kernel(bounds_ref, packed_ref, out_ref):
    blocks, _, rows, _ = packed_ref.shape
    slab = blocks * rows
    first, second = bounds_ref[0], bounds_ref[1]
    factor = math.log2(math.e) / math.sqrt(HDIM)

    def start_of(position):
        return jnp.where(position >= second, second, jnp.where(position >= first, first, 0))

    def tokens(index, start, count):
        return packed_ref[pl.ds(start // rows, count // rows), index].reshape(count, HDIM)

    def values_t(start, count):
        part = packed_ref[pl.ds(start // rows, count // rows), 2]
        return jnp.concatenate([part[i] for i in range(count // rows)], axis=1)

    def attend(state, query, keys, v_t, mask):
        scores = lax.dot_general(keys, query, (((1,), (1,)), ((), ())), preferred_element_type=jnp.float32)
        if mask is not None:
            scores = jnp.where(mask, scores, MASKED)
        top = jnp.max(scores, axis=0, keepdims=True)
        if state is not None:
            top = jnp.maximum(state[0], top)
        weights = jnp.exp2((scores - top) * factor)
        total = jnp.sum(weights, axis=0, keepdims=True)
        accum = jnp.dot(v_t, weights.astype(jnp.bfloat16), preferred_element_type=jnp.float32)
        if state is not None:
            rescale = jnp.exp2((state[0] - top) * factor)
            total = total + state[1] * rescale
            accum = accum + state[2] * rescale
        return top, total, accum

    for tile in range(slab // TILE):
        base = tile * TILE
        query = tokens(0, base, TILE)
        position = base + lax.broadcasted_iota(jnp.int32, (1, TILE), 1)
        starts = start_of(position)
        key_pos = base + lax.broadcasted_iota(jnp.int32, (TILE, 1), 0)
        mask = (key_pos <= position) & (key_pos >= starts)
        state = attend(None, query, tokens(1, base, TILE), values_t(base, TILE), mask)
        if tile:
            begin = start_of(jnp.int32(base))
            low = begin // TILE
            full = jnp.minimum((start_of(jnp.int32(base + TILE - 1)) + TILE - 1) // TILE, tile)
            ends = jnp.minimum(
                jnp.where(first > base, first, slab), jnp.where(second > base, second, slab)
            )
            narrow = ends - base <= HALF
            short = jnp.logical_not(narrow) & (low < full) & (begin - low * TILE >= HALF)
            short = short.astype(jnp.int32)

            def masked(state, query, start, count, starts):
                mask = start + lax.broadcasted_iota(jnp.int32, (count, 1), 0) >= starts
                return attend(state, query, tokens(1, start, count), values_t(start, count), mask)

            def whole(j, state):
                start = pl.multiple_of(j * TILE, TILE)
                return attend(state, query, tokens(1, start, TILE), values_t(start, TILE), None)

            def wide(j, state):
                return masked(state, query, pl.multiple_of(j * TILE, TILE), TILE, starts)

            def second_half(_, state):
                return masked(state, query, pl.multiple_of(low * TILE + HALF, HALF), HALF, starts)

            def first_queries(j, state):
                part = tuple(item[:, :HALF] for item in state)
                start = pl.multiple_of(j * TILE, TILE)
                part = masked(part, query[:HALF], start, TILE, starts[:, :HALF])
                return tuple(
                    jnp.concatenate([new, old[:, HALF:]], axis=1) for new, old in zip(part, state)
                )

            state = lax.fori_loop(full, tile, whole, state)
            state = lax.fori_loop(low + short, jnp.where(narrow, low, full), wide, state)
            state = lax.fori_loop(0, short, second_half, state)
            state = lax.fori_loop(low, jnp.where(narrow, full, low), first_queries, state)
        _, total, accum = state
        finished = jnp.transpose((accum / total).astype(jnp.bfloat16))
        out_ref[base // rows:(base + TILE) // rows] = finished.reshape(TILE // rows, rows, HDIM)


def pack_kernel(queries_ref, keys_ref, values_ref, out_ref):
    for head in range(out_ref.shape[0]):
        columns = slice(head * HDIM, (head + 1) * HDIM)
        out_ref[head, 0] = queries_ref[:, columns]
        out_ref[head, 1] = keys_ref[:, columns]
        out_ref[head, 2] = jnp.transpose(values_ref[:, columns])


def pack(queries, keys, values):
    rows, width = queries.shape
    heads = width // HDIM
    half = pl.BlockSpec((rows, width // 2), lambda i: (0, i))
    return pl.pallas_call(
        pack_kernel,
        out_shape=jax.ShapeDtypeStruct((heads, 3, rows, HDIM), queries.dtype),
        grid=(2,),
        in_specs=[half] * 3,
        out_specs=pl.BlockSpec((heads // 2, 3, rows, HDIM), lambda i: (i, 0, 0, 0)),
        name="pack",
    )(queries, keys, values)


def head_attention(bounds, packed):
    blocks, _, rows, _ = packed.shape
    vmem = pl.BlockSpec(memory_space=pltpu.VMEM)
    return pl.pallas_call(
        attention_kernel,
        out_shape=jax.ShapeDtypeStruct((blocks, rows, HDIM), jnp.bfloat16),
        in_specs=[pl.BlockSpec(memory_space=pltpu.SMEM), vmem],
        out_specs=vmem,
        compiler_params=pltpu.CompilerParams(vmem_limit_bytes=16 << 20),
        name="head_attention",
    )(bounds, packed)


def projection_kernel(places, place_ref, mine_ref, theirs_ref, *rest):
    pieces = rest[:-7]
    out_ref, sent_ref, kept_ref, left_ref, weight_ref, weight_semaphores, semaphores = rest[-7:]
    columns = sent_ref.shape[1]
    rows = mine_ref.shape[1]
    loads = []
    for strip in range(columns // STRIP):
        at = 0
        for i, piece in enumerate(pieces):
            count = piece.shape[0]
            source = piece.at[:, :, strip * STRIP:(strip + 1) * STRIP]
            target = weight_ref.at[strip, pl.ds(at, count)]
            loads.append(pltpu.make_async_copy(source, target, weight_semaphores.at[strip, i]))
            loads[-1].start()
            at += count
    y, x, core = place_ref[0], place_ref[1], place_ref[2]
    for i, (far, near) in enumerate(places):
        dy = jnp.where(core == 0, far, near)
        dx = jnp.where(core == 0, near, far)
        head = ((y + dy) % SIDE) * SIDE + (x + dx) % SIDE
        left_ref[:rows, i * HDIM:(i + 1) * HDIM] = mine_ref[head]
        left_ref[rows:, i * HDIM:(i + 1) * HDIM] = theirs_ref[head]
    copies = []
    for strip in range(columns // STRIP):
        at = slice(strip * STRIP, (strip + 1) * STRIP)
        for load in loads[strip * len(pieces):(strip + 1) * len(pieces)]:
            load.wait()
        result = jnp.dot(
            left_ref[...],
            weight_ref[strip].reshape(len(places) * HDIM, STRIP),
            preferred_element_type=jnp.float32,
        ).astype(jnp.bfloat16)
        sent_ref[:, at] = result[rows:]
        kept_ref[strip] = result[:rows]
        target = pl.multiple_of(core * columns + strip * STRIP, STRIP)
        copies.append(
            pltpu.make_async_copy(
                kept_ref.at[strip], out_ref.at[:, pl.ds(target, STRIP)], semaphores.at[strip]
            )
        )
        copies[-1].start()
    for copy in copies:
        copy.wait()


def project(place, mine, theirs, pieces, places):
    heads, rows, _ = mine.shape
    columns = pieces[0].shape[2]
    strips = columns // STRIP
    vmem = pl.BlockSpec(memory_space=pltpu.VMEM)
    hbm = pl.BlockSpec(memory_space=pltpu.HBM)
    pieces = [pltpu.with_memory_space_constraint(piece, pltpu.HBM) for piece in pieces]
    return pl.pallas_call(
        functools.partial(projection_kernel, places),
        out_shape=(
            jax.ShapeDtypeStruct((rows, 2 * columns), jnp.bfloat16),
            jax.ShapeDtypeStruct((rows, columns), jnp.bfloat16),
        ),
        in_specs=[pl.BlockSpec(memory_space=pltpu.SMEM), vmem, vmem] + [hbm] * len(pieces),
        out_specs=(hbm, vmem),
        scratch_shapes=[
            pltpu.VMEM((strips, rows, STRIP), jnp.bfloat16),
            pltpu.VMEM((2 * rows, heads * HDIM), jnp.bfloat16),
            pltpu.VMEM((strips, heads, HDIM, STRIP), jnp.bfloat16),
            pltpu.SemaphoreType.DMA((strips, len(pieces))),
            pltpu.SemaphoreType.DMA((strips,)),
        ],
        compiler_params=pltpu.CompilerParams(vmem_limit_bytes=20 << 20),
        name="project",
    )(place, mine, theirs, *pieces)


def fetch(piece, step, near):
    count = lax.axis_size("ctx")
    pairs = []
    for y in range(SIDE):
        for x in range(SIDE):
            for place in range(count):
                along_x = (place % 2 == 0) == near
                source_y = y if along_x else (y + step) % SIDE
                source_x = (x + step) % SIDE if along_x else x
                pairs.append(
                    ((SIDE * source_y + source_x) * count + place, (SIDE * y + x) * count + place)
                )
    return lax.ppermute(piece, ("fsdp", "ctx"), pairs)


def per_device(queries, keys, values, out_weight, sessions):
    core = lax.axis_index("ctx") % 2
    swap = [(i, i ^ 1) for i in range(lax.axis_size("ctx"))]
    bounds = jnp.stack([jnp.sum(sessions[0] < 1), jnp.sum(sessions[0] < 2)]).astype(jnp.int32)
    place = lax.axis_index("fsdp")
    place = jnp.stack([place // SIDE, place % SIDE, core]).astype(jnp.int32)

    packed = lax.all_to_all(pack(queries, keys, values), "ctx", 0, 0, tiled=True)

    half = out_weight.shape[1] // 2
    own = lax.dynamic_slice_in_dim(out_weight, core * half, half, 1)
    line = jnp.stack([own] + [fetch(own, step, True) for step in NEAR[1:]])
    packed, _ = lax.optimization_barrier((packed, line))
    pieces = [line] + [fetch(line, step, False) for step in NEAR[1:]]
    places = [(far, near) for far in NEAR for near in NEAR]
    attended = head_attention(bounds, packed)
    mine = lax.all_to_all(attended, "ctx", 0, 0, tiled=True)
    theirs = lax.ppermute(mine, "ctx", swap)
    part, sent = project(place, mine, theirs, pieces, places)
    got = lax.ppermute(sent, "ctx", swap)
    return lax.dynamic_update_slice(part, got, (0, (1 - core) * half))


def solution(mesh):
    return jax.shard_map(
        per_device,
        mesh=mesh,
        in_specs=(
            P(("fsdp", "ctx"), None),
            P(("fsdp", "ctx"), None),
            P(("fsdp", "ctx"), None),
            P("fsdp", None),
            P("fsdp", None),
        ),
        out_specs=P(("fsdp", "ctx"), None),
        check_vma=False,
    )
```

```python
import functools
import math

import jax
import jax.numpy as jnp
from jax import lax
from jax.experimental import pallas as pl
from jax.experimental.pallas import tpu as pltpu
from jax.sharding import PartitionSpec as P

HDIM = 128
TILE = 512
HALF = TILE // 2
MASKED = -1e30
SIDE = 4
NEAR = (0, 1, 3, 2)
STRIP = 512


def attention_kernel(bounds_ref, packed_ref, out_ref):
    blocks, _, rows, _ = packed_ref.shape
    slab = blocks * rows
    first, second = bounds_ref[0], bounds_ref[1]
    factor = math.log2(math.e) / math.sqrt(HDIM)

    def start_of(position):
        return jnp.where(position >= second, second, jnp.where(position >= first, first, 0))

    def tokens(index, start, count):
        return packed_ref[pl.ds(start // rows, count // rows), index].reshape(count, HDIM)

    def values_t(start, count):
        part = packed_ref[pl.ds(start // rows, count // rows), 2]
        return jnp.concatenate([part[i] for i in range(count // rows)], axis=1)

    def attend(state, query, keys, v_t, mask):
        scores = lax.dot_general(keys, query, (((1,), (1,)), ((), ())), preferred_element_type=jnp.float32)
        if mask is not None:
            scores = jnp.where(mask, scores, MASKED)
        top = jnp.max(scores, axis=0, keepdims=True)
        if state is not None:
            top = jnp.maximum(state[0], top)
        weights = jnp.exp2((scores - top) * factor)
        total = jnp.sum(weights, axis=0, keepdims=True)
        accum = jnp.dot(v_t, weights.astype(jnp.bfloat16), preferred_element_type=jnp.float32)
        if state is not None:
            rescale = jnp.exp2((state[0] - top) * factor)
            total = total + state[1] * rescale
            accum = accum + state[2] * rescale
        return top, total, accum

    for tile in range(slab // TILE):
        base = tile * TILE
        query = tokens(0, base, TILE)
        position = base + lax.broadcasted_iota(jnp.int32, (1, TILE), 1)
        starts = start_of(position)
        key_pos = base + lax.broadcasted_iota(jnp.int32, (TILE, 1), 0)
        mask = (key_pos <= position) & (key_pos >= starts)
        state = attend(None, query, tokens(1, base, TILE), values_t(base, TILE), mask)
        if tile:
            begin = start_of(jnp.int32(base))
            low = begin // TILE
            full = jnp.minimum((start_of(jnp.int32(base + TILE - 1)) + TILE - 1) // TILE, tile)
            ends = jnp.minimum(
                jnp.where(first > base, first, slab), jnp.where(second > base, second, slab)
            )
            narrow = ends - base <= HALF
            short = jnp.logical_not(narrow) & (low < full) & (begin - low * TILE >= HALF)
            short = short.astype(jnp.int32)

            def masked(state, query, start, count, starts):
                mask = start + lax.broadcasted_iota(jnp.int32, (count, 1), 0) >= starts
                return attend(state, query, tokens(1, start, count), values_t(start, count), mask)

            def whole(j, state):
                start = pl.multiple_of(j * TILE, TILE)
                return attend(state, query, tokens(1, start, TILE), values_t(start, TILE), None)

            def wide(j, state):
                return masked(state, query, pl.multiple_of(j * TILE, TILE), TILE, starts)

            def second_half(_, state):
                return masked(state, query, pl.multiple_of(low * TILE + HALF, HALF), HALF, starts)

            def first_queries(j, state):
                part = tuple(item[:, :HALF] for item in state)
                start = pl.multiple_of(j * TILE, TILE)
                part = masked(part, query[:HALF], start, TILE, starts[:, :HALF])
                return tuple(
                    jnp.concatenate([new, old[:, HALF:]], axis=1) for new, old in zip(part, state)
                )

            state = lax.fori_loop(full, tile, whole, state)
            state = lax.fori_loop(low + short, jnp.where(narrow, low, full), wide, state)
            state = lax.fori_loop(0, short, second_half, state)
            state = lax.fori_loop(low, jnp.where(narrow, full, low), first_queries, state)
        _, total, accum = state
        finished = jnp.transpose((accum / total).astype(jnp.bfloat16))
        out_ref[base // rows:(base + TILE) // rows] = finished.reshape(TILE // rows, rows, HDIM)


def pack_kernel(queries_ref, keys_ref, values_ref, out_ref):
    for head in range(out_ref.shape[0]):
        columns = slice(head * HDIM, (head + 1) * HDIM)
        out_ref[head, 0] = queries_ref[:, columns]
        out_ref[head, 1] = keys_ref[:, columns]
        out_ref[head, 2] = jnp.transpose(values_ref[:, columns])


def pack(queries, keys, values):
    rows, width = queries.shape
    heads = width // HDIM
    half = pl.BlockSpec((rows, width // 2), lambda i: (0, i))
    return pl.pallas_call(
        pack_kernel,
        out_shape=jax.ShapeDtypeStruct((heads, 3, rows, HDIM), queries.dtype),
        grid=(2,),
        in_specs=[half] * 3,
        out_specs=pl.BlockSpec((heads // 2, 3, rows, HDIM), lambda i: (i, 0, 0, 0)),
        name="pack",
    )(queries, keys, values)


def head_attention(bounds, packed):
    blocks, _, rows, _ = packed.shape
    vmem = pl.BlockSpec(memory_space=pltpu.VMEM)
    return pl.pallas_call(
        attention_kernel,
        out_shape=jax.ShapeDtypeStruct((blocks, rows, HDIM), jnp.bfloat16),
        in_specs=[pl.BlockSpec(memory_space=pltpu.SMEM), vmem],
        out_specs=vmem,
        compiler_params=pltpu.CompilerParams(vmem_limit_bytes=16 << 20),
        name="head_attention",
    )(bounds, packed)


def projection_kernel(places, place_ref, mine_ref, theirs_ref, *rest):
    pieces = rest[:-7]
    out_ref, sent_ref, kept_ref, left_ref, weight_ref, weight_semaphores, semaphores = rest[-7:]
    columns = sent_ref.shape[1]
    rows = mine_ref.shape[1]
    loads = []
    for strip in range(columns // STRIP):
        at = 0
        for i, piece in enumerate(pieces):
            count = piece.shape[0]
            source = piece.at[:, :, strip * STRIP:(strip + 1) * STRIP]
            target = weight_ref.at[strip, pl.ds(at, count)]
            loads.append(pltpu.make_async_copy(source, target, weight_semaphores.at[strip, i]))
            loads[-1].start()
            at += count
    y, x, core = place_ref[0], place_ref[1], place_ref[2]
    for i, (far, near) in enumerate(places):
        dy = jnp.where(core == 1, far, near)
        dx = jnp.where(core == 1, near, far)
        head = ((y + dy) % SIDE) * SIDE + (x + dx) % SIDE
        left_ref[:rows, i * HDIM:(i + 1) * HDIM] = mine_ref[head]
        left_ref[rows:, i * HDIM:(i + 1) * HDIM] = theirs_ref[head]
    copies = []
    for strip in range(columns // STRIP):
        at = slice(strip * STRIP, (strip + 1) * STRIP)
        for load in loads[strip * len(pieces):(strip + 1) * len(pieces)]:
            load.wait()
        result = jnp.dot(
            left_ref[...],
            weight_ref[strip].reshape(len(places) * HDIM, STRIP),
            preferred_element_type=jnp.float32,
        ).astype(jnp.bfloat16)
        sent_ref[:, at] = result[rows:]
        kept_ref[strip] = result[:rows]
        target = pl.multiple_of(core * columns + strip * STRIP, STRIP)
        copies.append(
            pltpu.make_async_copy(
                kept_ref.at[strip], out_ref.at[:, pl.ds(target, STRIP)], semaphores.at[strip]
            )
        )
        copies[-1].start()
    for copy in copies:
        copy.wait()


def project(place, mine, theirs, pieces, places):
    heads, rows, _ = mine.shape
    columns = pieces[0].shape[2]
    strips = columns // STRIP
    vmem = pl.BlockSpec(memory_space=pltpu.VMEM)
    hbm = pl.BlockSpec(memory_space=pltpu.HBM)
    pieces = [pltpu.with_memory_space_constraint(piece, pltpu.HBM) for piece in pieces]
    return pl.pallas_call(
        functools.partial(projection_kernel, places),
        out_shape=(
            jax.ShapeDtypeStruct((rows, 2 * columns), jnp.bfloat16),
            jax.ShapeDtypeStruct((rows, columns), jnp.bfloat16),
        ),
        in_specs=[pl.BlockSpec(memory_space=pltpu.SMEM), vmem, vmem] + [hbm] * len(pieces),
        out_specs=(hbm, vmem),
        scratch_shapes=[
            pltpu.VMEM((strips, rows, STRIP), jnp.bfloat16),
            pltpu.VMEM((2 * rows, heads * HDIM), jnp.bfloat16),
            pltpu.VMEM((strips, heads, HDIM, STRIP), jnp.bfloat16),
            pltpu.SemaphoreType.DMA((strips, len(pieces))),
            pltpu.SemaphoreType.DMA((strips,)),
        ],
        compiler_params=pltpu.CompilerParams(vmem_limit_bytes=20 << 20),
        name="project",
    )(place, mine, theirs, *pieces)


def fetch(piece, step, near):
    count = lax.axis_size("ctx")
    pairs = []
    for y in range(SIDE):
        for x in range(SIDE):
            for place in range(count):
                along_x = (place % 2 == 1) == near
                source_y = y if along_x else (y + step) % SIDE
                source_x = (x + step) % SIDE if along_x else x
                pairs.append(
                    ((SIDE * source_y + source_x) * count + place, (SIDE * y + x) * count + place)
                )
    return lax.ppermute(piece, ("fsdp", "ctx"), pairs)


def per_device(queries, keys, values, out_weight, sessions):
    core = lax.axis_index("ctx") % 2
    swap = [(i, i ^ 1) for i in range(lax.axis_size("ctx"))]
    bounds = jnp.stack([jnp.sum(sessions[0] < 1), jnp.sum(sessions[0] < 2)]).astype(jnp.int32)
    place = lax.axis_index("fsdp")
    place = jnp.stack([place // SIDE, place % SIDE, core]).astype(jnp.int32)

    packed = lax.all_to_all(pack(queries, keys, values), "ctx", 0, 0, tiled=True)

    half = out_weight.shape[1] // 2
    own = lax.dynamic_slice_in_dim(out_weight, core * half, half, 1)
    line = jnp.stack([own] + [fetch(own, step, True) for step in NEAR[1:]])
    packed, _ = lax.optimization_barrier((packed, line))
    pieces = [line] + [fetch(line, step, False) for step in NEAR[1:]]
    places = [(far, near) for far in NEAR for near in NEAR]
    attended = head_attention(bounds, packed)
    mine = lax.all_to_all(attended, "ctx", 0, 0, tiled=True)
    theirs = lax.ppermute(mine, "ctx", swap)
    part, sent = project(place, mine, theirs, pieces, places)
    got = lax.ppermute(sent, "ctx", swap)
    return lax.dynamic_update_slice(part, got, (0, (1 - core) * half))


def solution(mesh):
    return jax.shard_map(
        per_device,
        mesh=mesh,
        in_specs=(
            P(("fsdp", "ctx"), None),
            P(("fsdp", "ctx"), None),
            P(("fsdp", "ctx"), None),
            P("fsdp", None),
            P("fsdp", None),
        ),
        out_specs=P(("fsdp", "ctx"), None),
        check_vma=False,
    )
```

```python
import functools
import math

import jax
import jax.numpy as jnp
from jax import lax
from jax.experimental import pallas as pl
from jax.experimental.pallas import tpu as pltpu
from jax.sharding import PartitionSpec as P

HDIM = 128
TILE = 512
HALF = TILE // 2
MASKED = -1e30
SIDE = 4
NEAR = (0, 1, 2, 3)
STRIP = 512


def attention_kernel(bounds_ref, packed_ref, out_ref):
    blocks, _, rows, _ = packed_ref.shape
    slab = blocks * rows
    first, second = bounds_ref[0], bounds_ref[1]
    factor = math.log2(math.e) / math.sqrt(HDIM)

    def start_of(position):
        return jnp.where(position >= second, second, jnp.where(position >= first, first, 0))

    def tokens(index, start, count):
        return packed_ref[pl.ds(start // rows, count // rows), index].reshape(count, HDIM)

    def values_t(start, count):
        part = packed_ref[pl.ds(start // rows, count // rows), 2]
        return jnp.concatenate([part[i] for i in range(count // rows)], axis=1)

    def attend(state, query, keys, v_t, mask):
        scores = lax.dot_general(keys, query, (((1,), (1,)), ((), ())), preferred_element_type=jnp.float32)
        if mask is not None:
            scores = jnp.where(mask, scores, MASKED)
        top = jnp.max(scores, axis=0, keepdims=True)
        if state is not None:
            top = jnp.maximum(state[0], top)
        weights = jnp.exp2((scores - top) * factor)
        total = jnp.sum(weights, axis=0, keepdims=True)
        accum = jnp.dot(v_t, weights.astype(jnp.bfloat16), preferred_element_type=jnp.float32)
        if state is not None:
            rescale = jnp.exp2((state[0] - top) * factor)
            total = total + state[1] * rescale
            accum = accum + state[2] * rescale
        return top, total, accum

    for tile in range(slab // TILE):
        base = tile * TILE
        query = tokens(0, base, TILE)
        position = base + lax.broadcasted_iota(jnp.int32, (1, TILE), 1)
        starts = start_of(position)
        key_pos = base + lax.broadcasted_iota(jnp.int32, (TILE, 1), 0)
        mask = (key_pos <= position) & (key_pos >= starts)
        state = attend(None, query, tokens(1, base, TILE), values_t(base, TILE), mask)
        if tile:
            begin = start_of(jnp.int32(base))
            low = begin // TILE
            full = jnp.minimum((start_of(jnp.int32(base + TILE - 1)) + TILE - 1) // TILE, tile)
            ends = jnp.minimum(
                jnp.where(first > base, first, slab), jnp.where(second > base, second, slab)
            )
            narrow = ends - base <= HALF
            short = jnp.logical_not(narrow) & (low < full) & (begin - low * TILE >= HALF)
            short = short.astype(jnp.int32)

            def masked(state, query, start, count, starts):
                mask = start + lax.broadcasted_iota(jnp.int32, (count, 1), 0) >= starts
                return attend(state, query, tokens(1, start, count), values_t(start, count), mask)

            def whole(j, state):
                start = pl.multiple_of(j * TILE, TILE)
                return attend(state, query, tokens(1, start, TILE), values_t(start, TILE), None)

            def wide(j, state):
                return masked(state, query, pl.multiple_of(j * TILE, TILE), TILE, starts)

            def second_half(_, state):
                return masked(state, query, pl.multiple_of(low * TILE + HALF, HALF), HALF, starts)

            def first_queries(j, state):
                part = tuple(item[:, :HALF] for item in state)
                start = pl.multiple_of(j * TILE, TILE)
                part = masked(part, query[:HALF], start, TILE, starts[:, :HALF])
                return tuple(
                    jnp.concatenate([new, old[:, HALF:]], axis=1) for new, old in zip(part, state)
                )

            state = lax.fori_loop(full, tile, whole, state)
            state = lax.fori_loop(low + short, jnp.where(narrow, low, full), wide, state)
            state = lax.fori_loop(0, short, second_half, state)
            state = lax.fori_loop(low, jnp.where(narrow, full, low), first_queries, state)
        _, total, accum = state
        finished = jnp.transpose((accum / total).astype(jnp.bfloat16))
        out_ref[base // rows:(base + TILE) // rows] = finished.reshape(TILE // rows, rows, HDIM)


def pack_kernel(queries_ref, keys_ref, values_ref, out_ref):
    for head in range(out_ref.shape[0]):
        columns = slice(head * HDIM, (head + 1) * HDIM)
        out_ref[head, 0] = queries_ref[:, columns]
        out_ref[head, 1] = keys_ref[:, columns]
        out_ref[head, 2] = jnp.transpose(values_ref[:, columns])


def pack(queries, keys, values):
    rows, width = queries.shape
    heads = width // HDIM
    half = pl.BlockSpec((rows, width // 2), lambda i: (0, i))
    return pl.pallas_call(
        pack_kernel,
        out_shape=jax.ShapeDtypeStruct((heads, 3, rows, HDIM), queries.dtype),
        grid=(2,),
        in_specs=[half] * 3,
        out_specs=pl.BlockSpec((heads // 2, 3, rows, HDIM), lambda i: (i, 0, 0, 0)),
        name="pack",
    )(queries, keys, values)


def head_attention(bounds, packed):
    blocks, _, rows, _ = packed.shape
    vmem = pl.BlockSpec(memory_space=pltpu.VMEM)
    return pl.pallas_call(
        attention_kernel,
        out_shape=jax.ShapeDtypeStruct((blocks, rows, HDIM), jnp.bfloat16),
        in_specs=[pl.BlockSpec(memory_space=pltpu.SMEM), vmem],
        out_specs=vmem,
        compiler_params=pltpu.CompilerParams(vmem_limit_bytes=16 << 20),
        name="head_attention",
    )(bounds, packed)


def projection_kernel(places, place_ref, mine_ref, theirs_ref, *rest):
    pieces = rest[:-7]
    out_ref, sent_ref, kept_ref, left_ref, weight_ref, weight_semaphores, semaphores = rest[-7:]
    columns = sent_ref.shape[1]
    rows = mine_ref.shape[1]
    loads = []
    for strip in range(columns // STRIP):
        at = 0
        for i, piece in enumerate(pieces):
            count = piece.shape[0]
            source = piece.at[:, :, strip * STRIP:(strip + 1) * STRIP]
            target = weight_ref.at[strip, pl.ds(at, count)]
            loads.append(pltpu.make_async_copy(source, target, weight_semaphores.at[strip, i]))
            loads[-1].start()
            at += count
    y, x, core = place_ref[0], place_ref[1], place_ref[2]
    for i, (far, near) in enumerate(places):
        dy = jnp.where(core == 0, far, near)
        dx = jnp.where(core == 0, near, far)
        head = ((y + dy) % SIDE) * SIDE + (x + dx) % SIDE
        left_ref[:rows, i * HDIM:(i + 1) * HDIM] = mine_ref[head]
        left_ref[rows:, i * HDIM:(i + 1) * HDIM] = theirs_ref[head]
    copies = []
    for strip in range(columns // STRIP):
        at = slice(strip * STRIP, (strip + 1) * STRIP)
        for load in loads[strip * len(pieces):(strip + 1) * len(pieces)]:
            load.wait()
        result = jnp.dot(
            left_ref[...],
            weight_ref[strip].reshape(len(places) * HDIM, STRIP),
            preferred_element_type=jnp.float32,
        ).astype(jnp.bfloat16)
        sent_ref[:, at] = result[rows:]
        kept_ref[strip] = result[:rows]
        target = pl.multiple_of(core * columns + strip * STRIP, STRIP)
        copies.append(
            pltpu.make_async_copy(
                kept_ref.at[strip], out_ref.at[:, pl.ds(target, STRIP)], semaphores.at[strip]
            )
        )
        copies[-1].start()
    for copy in copies:
        copy.wait()


def project(place, mine, theirs, pieces, places):
    heads, rows, _ = mine.shape
    columns = pieces[0].shape[2]
    strips = columns // STRIP
    vmem = pl.BlockSpec(memory_space=pltpu.VMEM)
    hbm = pl.BlockSpec(memory_space=pltpu.HBM)
    pieces = [pltpu.with_memory_space_constraint(piece, pltpu.HBM) for piece in pieces]
    return pl.pallas_call(
        functools.partial(projection_kernel, places),
        out_shape=(
            jax.ShapeDtypeStruct((rows, 2 * columns), jnp.bfloat16),
            jax.ShapeDtypeStruct((rows, columns), jnp.bfloat16),
        ),
        in_specs=[pl.BlockSpec(memory_space=pltpu.SMEM), vmem, vmem] + [hbm] * len(pieces),
        out_specs=(hbm, vmem),
        scratch_shapes=[
            pltpu.VMEM((strips, rows, STRIP), jnp.bfloat16),
            pltpu.VMEM((2 * rows, heads * HDIM), jnp.bfloat16),
            pltpu.VMEM((strips, heads, HDIM, STRIP), jnp.bfloat16),
            pltpu.SemaphoreType.DMA((strips, len(pieces))),
            pltpu.SemaphoreType.DMA((strips,)),
        ],
        compiler_params=pltpu.CompilerParams(vmem_limit_bytes=20 << 20),
        name="project",
    )(place, mine, theirs, *pieces)


def fetch(piece, step, near):
    count = lax.axis_size("ctx")
    pairs = []
    for y in range(SIDE):
        for x in range(SIDE):
            for place in range(count):
                along_x = (place % 2 == 0) == near
                source_y = y if along_x else (y + step) % SIDE
                source_x = (x + step) % SIDE if along_x else x
                pairs.append(
                    ((SIDE * source_y + source_x) * count + place, (SIDE * y + x) * count + place)
                )
    return lax.ppermute(piece, ("fsdp", "ctx"), pairs)


def per_device(queries, keys, values, out_weight, sessions):
    core = lax.axis_index("ctx") % 2
    swap = [(i, i ^ 1) for i in range(lax.axis_size("ctx"))]
    bounds = jnp.stack([jnp.sum(sessions[0] < 1), jnp.sum(sessions[0] < 2)]).astype(jnp.int32)
    place = lax.axis_index("fsdp")
    place = jnp.stack([place // SIDE, place % SIDE, core]).astype(jnp.int32)

    packed = lax.all_to_all(pack(queries, keys, values), "ctx", 0, 0, tiled=True)

    half = out_weight.shape[1] // 2
    own = lax.dynamic_slice_in_dim(out_weight, core * half, half, 1)
    line = jnp.stack([own] + [fetch(own, step, True) for step in NEAR[1:]])
    packed, _ = lax.optimization_barrier((packed, line))
    pieces = [line] + [fetch(line, step, False) for step in NEAR[1:]]
    places = [(far, near) for far in NEAR for near in NEAR]
    attended = head_attention(bounds, packed)
    mine = lax.all_to_all(attended, "ctx", 0, 0, tiled=True)
    theirs = lax.ppermute(mine, "ctx", swap)
    part, sent = project(place, mine, theirs, pieces, places)
    got = lax.ppermute(sent, "ctx", swap)
    return lax.dynamic_update_slice(part, got, (0, (1 - core) * half))


def solution(mesh):
    return jax.shard_map(
        per_device,
        mesh=mesh,
        in_specs=(
            P(("fsdp", "ctx"), None),
            P(("fsdp", "ctx"), None),
            P(("fsdp", "ctx"), None),
            P("fsdp", None),
            P("fsdp", None),
        ),
        out_specs=P(("fsdp", "ctx"), None),
        check_vma=False,
    )
```
